256 devices in a mesh: dp: 8 (over z), bin: 32 (over x, y, core).
Axes of the slice: x: 4, y: 4, z: 8, core: 2. Of those that a mesh axis runs over, the one named last changes fastest.
Arguments:
- embeddings: bfloat16 [196608, 256], P(('dp', 'bin')), may hold values from -8 to 8
- bin_ids: int32 [196608], P(('dp', 'bin')), may hold values from 0 to 31, as said below
- spreads: float32 [3], replicated, may hold values from 0.5 to 4
- projection: bfloat16 [256, 256], replicated, may hold values from -0.375 to 0.375
Outputs:
- grad_emb: bfloat16 [196608, 256], P(('dp', 'bin'))
- grad_w: float32 [256, 256], replicated
- loss: float32 [], replicated
The draws below stay inside these ranges and needn't reach their ends.
Inputs may be any that keep to these rules, and one draw needn't show every extreme that they name: `bin_ids`: among the 768 jets of one device at most 48 share a mass bin, and on every device one bin holds exactly 48 of them.
All inputs are finite; a program needn't handle non-finite values.
Results may differ from the reference program's by a relative error of at most 0.0044.
The reference program's roundings to bfloat16 on the way count: a program that leaves them out, or rounds other values in their place, can miss the bound.
Values may be sent and summed in bfloat16 or wider, within the bound.
A program may use at most 64 MiB of HBM per device.

```python
import math
import jax
import jax.numpy as jnp
from jax import lax

D = 256
NSIG = 3
ROWS_DEV = 768
SEND_CAP = 48
TOKENS = 196608
N_DP = 8
N_BIN = 32


def shared_bins(key):
    blocks = TOKENS // ROWS_DEV
    keys = jax.random.split(jax.random.fold_in(key, 7), blocks)

    def one_block(block_key):
        first, second, third = jax.random.split(block_key, 3)
        heavy = jax.random.randint(first, (), 0, N_BIN)
        others = jax.random.permutation(second, (N_BIN - 1) * SEND_CAP)[:ROWS_DEV - SEND_CAP] // SEND_CAP
        others = others + (others >= heavy).astype(others.dtype)
        rows = jnp.concatenate([jnp.full((SEND_CAP,), heavy, others.dtype), others])
        return jax.random.permutation(third, rows)
    return jax.vmap(one_block)(keys).reshape(-1).astype(jnp.int32)


def draw_bin_ids(key, part):
    return shared_bins(key)


def draw_embeddings(key, part):
    bins = shared_bins(key)
    first, second = jax.random.split(jax.random.fold_in(key, 11), 2)
    offsets = 0.6 * jax.random.normal(first, (N_BIN, D), jnp.float32)
    values = jax.random.normal(second, (TOKENS, D), jnp.float32) + offsets[bins]
    return jnp.clip(values, -8.0, 8.0).astype(jnp.bfloat16)


def noise(key, shape, scale, most, kind=jnp.bfloat16):
    return jnp.clip(scale * jax.random.normal(key, shape, jnp.float32), -most, most).astype(kind)


def setup_inputs(seed: int = 0) -> dict:
    key_list = jax.random.split(jax.random.key(seed), 5)
    embeddings = draw_embeddings(jax.random.fold_in(key_list[4], 71), 0)
    bin_ids = draw_bin_ids(jax.random.fold_in(key_list[4], 71), 0)
    spreads = jnp.clip(jnp.exp(jax.random.uniform(key_list[2], (NSIG,), jnp.float32, math.log(0.5), math.log(4.0))), 0.5, 4.0)
    projection = noise(key_list[3], (D, D), D ** -0.5, 0.375)
    return {"embeddings": embeddings, "bin_ids": bin_ids, "spreads": spreads, "projection": projection}


def tile_terms(xa, mask_a, xb, mask_b, inv_bw, want_b):
    rows_a, width = xa.shape
    rows_b = xb.shape[0]
    block = 512 if rows_a % 512 == 0 else rows_a
    count = rows_a // block
    sq_b = jnp.sum(jnp.square(xb.astype(jnp.float32)), 1)
    coef = inv_bw / width

    def step(carry, item):
        total, col_sum, back = carry
        xblk, mblk = item
        inner = lax.dot_general(xblk, xb, (((1,), (1,)), ((), ())), preferred_element_type=jnp.float32)
        sq_a = jnp.sum(jnp.square(xblk.astype(jnp.float32)), 1)
        dist = sq_a[:, None] + sq_b[None, :] - 2.0 * inner
        kern = jnp.zeros(dist.shape, jnp.float32)
        weight = jnp.zeros(dist.shape, jnp.float32)
        for index in range(coef.shape[0]):
            expo = jnp.exp(-dist * coef[index])
            kern = kern + expo
            weight = weight + coef[index] * expo
        pairs = mblk[:, None] * mask_b[None, :]
        total = total + jnp.sum(kern * pairs)
        gram = (weight * pairs).astype(jnp.bfloat16)
        gram_f = gram.astype(jnp.float32)
        part_a = xblk.astype(jnp.float32) * jnp.sum(gram_f, 1)[:, None] - jnp.dot(gram, xb, preferred_element_type=jnp.float32)
        if want_b:
            col_sum = col_sum + jnp.sum(gram_f, 0)
            back = back + lax.dot_general(gram, xblk, (((0,), (0,)), ((), ())), preferred_element_type=jnp.float32)
        return (total, col_sum, back), part_a

    init = (jnp.zeros((), jnp.float32), jnp.zeros((rows_b,), jnp.float32), jnp.zeros((rows_b, width), jnp.float32))
    (total, col_sum, back), parts = lax.scan(step, init, (xa.reshape(count, block, width), mask_a.reshape(count, block)))
    part_a = parts.reshape(rows_a, width)
    part_b = xb.astype(jnp.float32) * col_sum[:, None] - back
    return total, part_a, part_b


def reference(embeddings, bin_ids, spreads, projection):
    inv_bw = 1.0 / spreads
    feats = jnp.dot(embeddings, projection, preferred_element_type=jnp.float32).astype(jnp.bfloat16)
    jets = ROWS_DEV * N_BIN
    cap = 2 * ROWS_DEV
    half = N_BIN // 2
    scale = float(ROWS_DEV * D)

    def group_fn(args):
        group_z, group_ids = args
        order = jnp.argsort(group_ids, stable=True).astype(jnp.int32)
        sorted_z = group_z[order]
        padded = jnp.concatenate([sorted_z, jnp.zeros((cap, D), jnp.bfloat16)], 0)
        counts = jnp.sum((group_ids[:, None] == jnp.arange(N_BIN, dtype=jnp.int32)[None, :]).astype(jnp.int32), 0)
        starts = (jnp.cumsum(counts) - counts).astype(jnp.int32)

        def bin_rows(which):
            rows = lax.dynamic_slice_in_dim(padded, starts[which].astype(jnp.int32), cap, 0)
            live = (jnp.arange(cap, dtype=jnp.int32) < counts[which]).astype(jnp.float32)
            return rows, live, jnp.maximum(counts[which].astype(jnp.float32), 1.0)

        def pair_fn(lower):
            xa, ma, na = bin_rows(lower)
            xc, mc, nc = bin_rows(lower + half)
            sa, pa, unused_a = tile_terms(xa, ma, xa, ma, inv_bw, False)
            sc, pc, unused_c = tile_terms(xc, mc, xc, mc, inv_bw, False)
            sx, pxa, pxc = tile_terms(xa, ma, xc, mc, inv_bw, True)
            grad_a = (scale * (-(4.0 / (na * na)) * pa + (4.0 / (na * nc)) * pxa)).astype(jnp.bfloat16)
            grad_c = (scale * (-(4.0 / (nc * nc)) * pc + (4.0 / (na * nc)) * pxc)).astype(jnp.bfloat16)
            pair_loss = sa / (na * na) + sc / (nc * nc) - 2.0 * sx / (na * nc)
            return grad_a, grad_c, pair_loss

        grad_a, grad_c, losses = lax.map(pair_fn, jnp.arange(half, dtype=jnp.int32))
        grads = jnp.concatenate([grad_a, grad_c], 0)
        slots = jnp.arange(cap, dtype=jnp.int32)
        places = starts[:, None] + slots[None, :]
        places = jnp.where(slots[None, :] < counts[:, None], places, jets).astype(jnp.int32)
        grad_sorted = jnp.zeros((jets + 1, D), jnp.bfloat16).at[places.reshape(-1)].set(grads.reshape(-1, D))[:jets]
        grad_group = jnp.zeros((jets, D), jnp.bfloat16).at[order].set(grad_sorted)
        return grad_group, jnp.sum(losses)

    grad_z, losses = lax.map(group_fn, (feats.reshape(N_DP, jets, D), bin_ids.reshape(N_DP, jets)))
    grad_z = grad_z.reshape(TOKENS, D)
    grad_emb = lax.dot_general(grad_z, projection, (((1,), (1,)), ((), ())), preferred_element_type=jnp.float32).astype(jnp.bfloat16)
    grad_w = lax.dot_general(embeddings, grad_z, (((0,), (0,)), ((), ())), preferred_element_type=jnp.float32) / TOKENS
    loss = jnp.sum(losses) / N_DP
    return grad_emb, grad_w, loss
```

```python
import functools
import math

import jax
import jax.numpy as jnp
from jax import lax
from jax.experimental import pallas as pl
from jax.experimental.pallas import tpu as pltpu
from jax.sharding import PartitionSpec as P

MESH = pl.DeviceIdType.MESH
F32 = jnp.float32
BF16 = jnp.bfloat16
FAR = 1e30
NT = (((1,), (1,)), ((), ()))
TN = (((0,), (0,)), ((), ()))


def iota(shape, dim):
    return lax.broadcasted_iota(jnp.int32, shape, dim)


def slot_places(ids, me, bins, cap):
    half = bins // 2
    jets = ids.shape[1]
    owner = jnp.where(ids >= half, 2 * (ids - half) + 1, 2 * ids)
    step = 256 if jets % 256 == 0 else jets
    before = jnp.where(iota((step, step), 0) < iota((step, step), 1), 1.0, 0.0).astype(BF16)
    wide = max(bins, 16)
    carry = jnp.zeros((wide, 1), F32)
    ranks = []
    for start in range(0, jets, step):
        hot = jnp.where(owner[:, start:start + step] == iota((wide, step), 0), 1.0, 0.0)
        seen = jnp.dot(hot.astype(BF16), before, preferred_element_type=F32) + carry
        ranks.append(jnp.sum(seen * hot, 0, keepdims=True))
        carry = carry + jnp.sum(hot, 1, keepdims=True)
    rank = jnp.concatenate(ranks, 1).astype(jnp.int32)
    away = owner - me
    away = jnp.where(away < 0, away + bins, away)
    return owner, away * cap + rank


def scatter_kernel(bins, cap, emb_ref, ids_ref, inbox, pinbox, counts, outbox, mine,
                   cnt_send, cnt_recv, send, recv, fwd_send, fwd_recv, loc):
    z, me = lax.axis_index("dp"), lax.axis_index("bin")
    sib = me + 1 - 2 * lax.rem(me, 2)
    jets = emb_ref.shape[0]
    barrier = pltpu.get_barrier_semaphore()
    for k in range(1, bins):
        pl.semaphore_signal(barrier, inc=1, device_id=(z, lax.rem(me + k, bins)), device_id_type=MESH)
    owner, place = slot_places(ids_ref[...], me, bins, cap)
    hot = jnp.where(owner == iota((128, jets), 0), 1.0, 0.0).astype(BF16)
    tally = lax.dot_general(jnp.ones((8, jets), BF16), hot, NT, preferred_element_type=F32)
    mine[...] = tally[0:1, :].astype(jnp.int32)
    counts[me] = tally[0:1, :].astype(jnp.int32)
    pl.semaphore_wait(barrier, bins - 1)

    def count_copy(k):
        return pltpu.make_async_remote_copy(
            src_ref=mine, dst_ref=counts.at[me], send_sem=cnt_send.at[k], recv_sem=cnt_recv.at[k],
            device_id=(z, lax.rem(me + k, bins)), device_id_type=MESH)

    def row_copy(k):
        return pltpu.make_async_remote_copy(
            src_ref=outbox.at[k], dst_ref=inbox.at[me], send_sem=send.at[k], recv_sem=recv.at[k],
            device_id=(z, lax.rem(me + k, bins)), device_id_type=MESH)

    for k in range(1, bins):
        count_copy(k).start()
    group = 8 if bins % 8 == 0 else bins
    emb = emb_ref[...]
    for first in range(0, bins, group):
        rows = group * cap
        pick = jnp.where(iota((rows, jets), 0) + first * cap == place, 1.0, 0.0).astype(BF16)
        block = jnp.dot(pick, emb, preferred_element_type=F32).astype(BF16)
        outbox[first:first + group] = block.reshape(group, cap, block.shape[1])
        for k in range(first, first + group):
            if k:
                row_copy(k).start()
    own = pltpu.make_async_copy(outbox.at[0], inbox.at[me], loc)
    own.start()

    def forward(src):
        return pltpu.make_async_remote_copy(
            src_ref=inbox.at[src], dst_ref=pinbox.at[src], send_sem=fwd_send, recv_sem=fwd_recv,
            device_id=(z, sib), device_id_type=MESH)

    own.wait()
    forward(me).start()
    for k in range(1, bins):
        row_copy(k).wait_recv()
        forward(lax.rem(me + bins - k, bins)).start()
    for k in range(1, bins):
        count_copy(k).wait()
        row_copy(k).wait_send()
    pltpu.make_async_remote_copy(
        src_ref=inbox, dst_ref=pinbox, send_sem=fwd_send, recv_sem=fwd_recv,
        device_id=(z, sib), device_id_type=MESH).wait()


def pair_kernel(bins, cap, br, bc, cnt_ref, spread_ref, proj_ref, mine_ref, other_ref, out_ref, w_ref,
                xs, ys, gs, fx, fy, sax, srx, sry, acc, rsum, tot):
    me = lax.axis_index("bin")
    width = proj_ref.shape[0]
    hw = width // 2
    sib = me + 1 - 2 * lax.rem(me, 2)

    def pack(src_ref, dst, column):
        off = 0
        for s in range(bins):
            rows = src_ref[s].astype(F32)
            dst[0, pl.ds(off, cap), :] = rows[:, :hw]
            dst[1, pl.ds(off, cap), :] = rows[:, hw:]
            off = off + cnt_ref[s, 0, column]
        dst[0, pl.ds(off, bc), :] = jnp.zeros((bc, hw), F32)
        dst[1, pl.ds(off, bc), :] = jnp.zeros((bc, hw), F32)
        return off

    n_own = pack(mine_ref, xs, me)
    n_oth = pack(other_ref, ys, sib)
    proj = proj_ref[...]
    ones = jnp.ones((8, width), BF16)

    def features(rows_ref, feat, col_sq, row_sq, n):
        def body(i, carry):
            base = pl.multiple_of(i * bc, bc)
            emb = jnp.concatenate([rows_ref[0, pl.ds(base, bc), :], rows_ref[1, pl.ds(base, bc), :]], 1).astype(BF16)
            val = jnp.dot(emb, proj, preferred_element_type=F32).astype(BF16)
            feat[pl.ds(base, bc), :] = val
            sq = jnp.square(val.astype(F32))
            high = sq.astype(BF16)
            low = (sq - high.astype(F32)).astype(BF16)
            line = lax.dot_general(ones, high, NT, preferred_element_type=F32)
            line = line + lax.dot_general(ones, low, NT, preferred_element_type=F32)
            row_sq[i] = jnp.where(iota((8, bc), 1) + base < n, line, FAR)
            if col_sq is not None:
                col = jnp.broadcast_to(jnp.sum(sq, 1, keepdims=True), (bc, 128))
                col_sq[pl.ds(base, bc), :] = jnp.where(iota((bc, 128), 0) + base < n, col, FAR)
            return carry
        blocks = (n + bc - 1) // bc
        lax.fori_loop(0, blocks, body, 0)
        return blocks

    cols_own = features(xs, fx, sax, srx, n_own)
    cols_oth = features(ys, fy, None, sry, n_oth)

    coef = [1.0 / jnp.full((1, bc), spread_ref[s], F32) / width for s in range(3)]
    rate = [c * math.log2(math.e) for c in coef]
    na = jnp.full((1, 128), jnp.maximum(n_own, 1).astype(F32), F32)
    nc = jnp.full((1, 128), jnp.maximum(n_oth, 1).astype(F32), F32)
    scale = float(bins * cap // 2 * width)
    k_self = scale * (-(4.0 / (na * na)))
    k_cross = scale * (4.0 / (na * nc))
    k_self = jnp.concatenate([k_self] * (width // 128), 1)
    k_cross = jnp.concatenate([k_cross] * (width // 128), 1)

    tot[...] = jnp.zeros_like(tot)
    w_ref[...] = jnp.zeros_like(w_ref)
    solid = jnp.ones((bc, 128), BF16)

    def row_block(i, carry):
        base = pl.multiple_of(i * br, br)
        xa = fx[pl.ds(base, br), :]
        xa2 = xa + xa
        sa = sax[pl.ds(base, br), :]
        sa = jnp.concatenate([sa] * (bc // 128), 1)

        def gather(which, feat, row_sq, blocks):
            acc[which] = jnp.zeros((br, width), F32)
            rsum[which] = jnp.zeros((br, 128), F32)

            def body(j, inner_carry):
                xb = feat[pl.ds(pl.multiple_of(j * bc, bc), bc), :]
                inner = lax.dot_general(xa2, xb, NT, preferred_element_type=F32)
                sb = row_sq[j]
                t = inner - sa - sb[0:1, :]
                e0 = jnp.exp2(t * rate[0])
                e1 = jnp.exp2(t * rate[1])
                e2 = jnp.exp2(t * rate[2])
                kern = e0 + e1 + e2
                tot[which] += jnp.sum(kern.reshape(br // 8, 8, bc), 0)
                gram = (e0 * coef[0] + e1 * coef[1] + e2 * coef[2]).astype(BF16)
                acc[which] += jnp.dot(gram, xb, preferred_element_type=F32)
                rsum[which] += jnp.dot(gram, solid, preferred_element_type=F32)
                return inner_carry
            lax.fori_loop(0, blocks, body, 0)
            total = jnp.concatenate([rsum[which]] * (width // 128), 1)
            return xa.astype(F32) * total - acc[which]

        p_self = gather(0, fx, srx, cols_own)
        p_cross = gather(1, fy, sry, cols_oth)
        gz = (k_self * p_self + k_cross * p_cross).astype(BF16)
        ge = lax.dot_general(gz, proj, NT, preferred_element_type=F32)
        gs[0, pl.ds(base, br), :] = ge[:, :hw]
        gs[1, pl.ds(base, br), :] = ge[:, hw:]
        emb = jnp.concatenate([xs[0, pl.ds(base, br), :], xs[1, pl.ds(base, br), :]], 1).astype(BF16)
        gw = lax.dot_general(emb, gz, TN, preferred_element_type=F32)
        w_ref[0, :width, :] += gw[:, :hw]
        w_ref[1, :width, :] += gw[:, hw:]
        return carry

    lax.fori_loop(0, (n_own + br - 1) // br, row_block, 0)
    gs[0, pl.ds(n_own, cap), :] = jnp.zeros((cap, hw), F32)
    gs[1, pl.ds(n_own, cap), :] = jnp.zeros((cap, hw), F32)
    line = jnp.sum(tot[0], 0, keepdims=True)[:, :128] if bc == 128 else sum(
        jnp.sum(tot[0], 0, keepdims=True)[:, p:p + 128] for p in range(0, bc, 128))
    cross = jnp.sum(tot[1], 0, keepdims=True)[:, :128] if bc == 128 else sum(
        jnp.sum(tot[1], 0, keepdims=True)[:, p:p + 128] for p in range(0, bc, 128))
    share = line / (na * na) - cross / (na * nc)
    for h in range(2):
        w_ref[h, width:width + 8, :] = jnp.broadcast_to(share, (8, 128))
    off = 0
    for s in range(bins):
        out_ref[s, :, :hw] = gs[0, pl.ds(off, cap), :].astype(BF16)
        out_ref[s, :, hw:] = gs[1, pl.ds(off, cap), :].astype(BF16)
        off = off + cnt_ref[s, 0, me]


def return_kernel(bins, reps, cap, slots, w_ref, ids_ref, g_out, w_out, l_out,
                  inbox, pick, p_recv, z_send, z_recv, a_send, a_recv, g_buf, zg, other,
                  send, recv, psem, zsem, asem, gsem, zgsem, fsem, loc):
    z, me = lax.axis_index("dp"), lax.axis_index("bin")
    core = lax.rem(me, 2)
    q = lax.div(me, 2)
    chips = bins // 2
    sib = me + 1 - 2 * core
    jets = g_out.shape[0]
    width = g_out.shape[1]
    zr = width // reps
    ar = zr // chips
    barrier = pltpu.get_barrier_semaphore()
    for k in range(1, bins):
        pl.semaphore_signal(barrier, inc=1, device_id=(z, lax.rem(me + k, bins)), device_id_type=MESH)
    for k in range(1, reps):
        pl.semaphore_signal(barrier, inc=1, device_id=(lax.rem(z + k, reps), me), device_id_type=MESH)
    pl.semaphore_wait(barrier, bins - 1 + reps - 1)

    def remote(src, dst, ssem, rsem, dev):
        return pltpu.make_async_remote_copy(
            src_ref=src, dst_ref=dst, send_sem=ssem, recv_sem=rsem, device_id=dev, device_id_type=MESH)

    pair = remote(w_ref.at[1 - core], p_recv, psem.at[0], psem.at[1], (z, sib))
    pair.start()

    def row_copy(k):
        dest = lax.rem(me + k, bins)
        return remote(slots.at[dest], inbox.at[bins - k], send, recv, (z, dest))

    for k in range(1, bins):
        row_copy(k).start()
    own = pltpu.make_async_copy(slots.at[me], inbox.at[0], loc)
    own.start()

    _, place = slot_places(ids_ref[...], me, bins, cap)
    for first in range(0, jets, 128 if jets % 128 == 0 else jets):
        size = min(128, jets - first)
        part = jnp.broadcast_to(place[:, first:first + size], (size, size))
        column = jnp.sum(jnp.where(iota((size, size), 0) == iota((size, size), 1), part, 0), 1, keepdims=True)
        pick[first:first + size, :] = jnp.where(column == iota((size, bins * cap), 1), 1.0, 0.0).astype(BF16)

    pair.wait()
    half = w_ref[core] + p_recv[...]
    loss_tile = half[width:width + 8, :]
    for k in range(reps):
        z_send[k, 0:zr, :] = half[k * zr:(k + 1) * zr, :]
        z_send[k, zr:zr + 8, :] = loss_tile

    def z_copy(k):
        dest = lax.rem(z + k, reps)
        return remote(z_send.at[dest], z_recv.at[z], zsem.at[0, k], zsem.at[1, k], (dest, me))

    for k in range(1, reps):
        z_copy(k).start()
    z_recv[z] = z_send[z]
    for k in range(1, reps):
        z_copy(k).wait()
    chunk = z_recv[0]
    for k in range(1, reps):
        chunk = chunk + z_recv[k]
    for k in range(chips):
        a_send[k, 0:ar, :] = chunk[k * ar:(k + 1) * ar, :]
        a_send[k, ar:ar + 1, :] = chunk[zr:zr + 1, :]

    def a_copy(k):
        dest = lax.rem(q + k, chips)
        return remote(a_send.at[dest], a_recv.at[q], asem.at[0, k], asem.at[1, k], (z, 2 * dest + core))

    for k in range(1, chips):
        a_copy(k).start()
    a_recv[q] = a_send[q]
    for k in range(1, chips):
        a_copy(k).wait()
    piece = a_recv[0, 0:ar + 1, :]
    for k in range(1, chips):
        piece = piece + a_recv[k, 0:ar + 1, :]
    l_out[...] = jnp.broadcast_to(jnp.sum(piece[ar:ar + 1, :], 1, keepdims=True) / reps, (1, 128))
    g_buf[q] = piece[0:ar, :]

    def g_copy(k):
        dest = lax.rem(q + k, chips)
        return remote(g_buf.at[q], g_buf.at[q], gsem.at[0, k], gsem.at[1, k], (z, 2 * dest + core))

    for k in range(1, chips):
        g_copy(k).start()
    for k in range(1, chips):
        g_copy(k).wait()
    for k in range(chips):
        zg[z, k * ar:(k + 1) * ar, :] = g_buf[k]

    def zg_copy(k):
        dest = lax.rem(z + k, reps)
        return remote(zg.at[z], zg.at[z], zgsem.at[0, k], zgsem.at[1, k], (dest, me))

    for k in range(1, reps):
        zg_copy(k).start()

    own.wait()
    remote(slots.at[pl.ds(0, bins - 1)], inbox.at[pl.ds(1, bins - 1)], send, recv, (z, sib)).wait()
    g_out[...] = jnp.dot(pick[...], inbox[...].reshape(bins * cap, width), preferred_element_type=F32).astype(BF16)

    for k in range(1, reps):
        zg_copy(k).wait()
    last = remote(zg, other, fsem.at[0], fsem.at[1], (z, sib))
    last.start()
    last.wait()
    tokens = float(jets * bins * reps)
    here = zg[...].reshape(width, 128) / tokens
    there = other[...].reshape(width, 128) / tokens
    w_out[:, 0:128] = jnp.where(core == 0, here, there)
    w_out[:, 128:256] = jnp.where(core == 0, there, here)


def vmem(count):
    return [pl.BlockSpec(memory_space=pltpu.VMEM)] * count


def local(embeddings, bin_ids, spreads, projection):
    jets, width = embeddings.shape
    bins, reps = lax.axis_size("bin"), lax.axis_size("dp")
    cap = 2 * jets // bins
    most = bins * cap
    chips = bins // 2
    ids = bin_ids.reshape(1, jets)
    dma = pltpu.SemaphoreType.DMA
    box = jax.ShapeDtypeStruct((bins, cap, width), BF16)
    limit = 48 << 20
    inbox, pinbox, counts = pl.pallas_call(
        functools.partial(scatter_kernel, bins, cap),
        out_shape=(box, box, jax.ShapeDtypeStruct((bins, 1, 128), jnp.int32)),
        in_specs=vmem(2), out_specs=tuple(vmem(3)),
        scratch_shapes=[
            pltpu.VMEM((bins, cap, width), BF16), pltpu.VMEM((1, 128), jnp.int32),
            dma((bins,)), dma((bins,)), dma((bins,)), dma((bins,)), dma, dma, dma],
        compiler_params=pltpu.CompilerParams(collective_id=0, has_side_effects=True, vmem_limit_bytes=limit),
        name="scatter",
    )(embeddings, ids)

    br, bc = 256, 256
    top = -(-most // bc) * bc
    room = top + bc
    slots, w_part = pl.pallas_call(
        functools.partial(pair_kernel, bins, cap, br, bc),
        out_shape=(box, jax.ShapeDtypeStruct((2, width + 8, 128), F32)),
        in_specs=[pl.BlockSpec(memory_space=pltpu.SMEM)] * 2 + vmem(3), out_specs=tuple(vmem(2)),
        scratch_shapes=[
            pltpu.VMEM((2, room, width // 2), F32), pltpu.VMEM((2, room, width // 2), F32),
            pltpu.VMEM((2, room, width // 2), F32),
            pltpu.VMEM((top, width), BF16), pltpu.VMEM((top, width), BF16),
            pltpu.VMEM((top, 128), F32), pltpu.VMEM((top // bc, 8, bc), F32), pltpu.VMEM((top // bc, 8, bc), F32),
            pltpu.VMEM((2, br, width), F32), pltpu.VMEM((2, br, 128), F32), pltpu.VMEM((2, 8, bc), F32)],
        compiler_params=pltpu.CompilerParams(vmem_limit_bytes=limit),
        name="pairs",
    )(counts, spreads, projection, inbox, pinbox)

    zr = width // reps
    ar = zr // chips
    ap = 4 if ar < 4 else ar + 8
    grad_emb, grad_w, loss = pl.pallas_call(
        functools.partial(return_kernel, bins, reps, cap),
        out_shape=(jax.ShapeDtypeStruct((jets, width), BF16), jax.ShapeDtypeStruct((width, width), F32),
                   jax.ShapeDtypeStruct((1, 128), F32)),
        in_specs=vmem(3), out_specs=tuple(vmem(3)),
        scratch_shapes=[
            pltpu.VMEM((bins, cap, width), BF16), pltpu.VMEM((jets, most), BF16),
            pltpu.VMEM((width + 8, 128), F32),
            pltpu.VMEM((reps, zr + 8, 128), F32), pltpu.VMEM((reps, zr + 8, 128), F32),
            pltpu.VMEM((chips, ap, 128), F32), pltpu.VMEM((chips, ap, 128), F32),
            pltpu.VMEM((chips, ar, 128), F32), pltpu.VMEM((reps, zr, 128), F32), pltpu.VMEM((reps, zr, 128), F32),
            dma, dma, dma((2,)), dma((2, reps)), dma((2, chips)), dma((2, chips)), dma((2, reps)), dma((2,)), dma],
        compiler_params=pltpu.CompilerParams(collective_id=1, has_side_effects=True, vmem_limit_bytes=limit),
        name="giveback",
    )(slots, w_part, ids)
    return grad_emb, grad_w, loss[0, 0]


def solution(mesh):
    return jax.shard_map(
        local,
        mesh=mesh,
        in_specs=(P(("dp", "bin"), None), P(("dp", "bin")), P(), P()),
        out_specs=(P(("dp", "bin"), None), P(), P()),
        check_vma=False,
    )
```

```python
import functools
import math

import jax
import jax.numpy as jnp
from jax import lax
from jax.experimental import pallas as pl
from jax.experimental.pallas import tpu as pltpu
from jax.sharding import PartitionSpec as P

MESH = pl.DeviceIdType.MESH
F32 = jnp.float32
BF16 = jnp.bfloat16
FAR = 1e30
STRIDE = 11
NT = (((1,), (1,)), ((), ()))
TN = (((0,), (0,)), ((), ()))


def iota(shape, dim):
    return lax.broadcasted_iota(jnp.int32, shape, dim)


def slot_places(ids, me, bins, cap):
    half = bins // 2
    jets = ids.shape[1]
    owner = jnp.where(ids >= half, 2 * (ids - half) + 1, 2 * ids)
    step = 256 if jets % 256 == 0 else jets
    before = jnp.where(iota((step, step), 0) < iota((step, step), 1), 1.0, 0.0).astype(BF16)
    wide = max(bins, 16)
    carry = jnp.zeros((wide, 1), F32)
    ranks = []
    for start in range(0, jets, step):
        hot = jnp.where(owner[:, start:start + step] == iota((wide, step), 0), 1.0, 0.0)
        seen = jnp.dot(hot.astype(BF16), before, preferred_element_type=F32) + carry
        ranks.append(jnp.sum(seen * hot, 0, keepdims=True))
        carry = carry + jnp.sum(hot, 1, keepdims=True)
    rank = jnp.concatenate(ranks, 1).astype(jnp.int32)
    away = owner - me
    away = jnp.where(away < 0, away + bins, away)
    turn = lax.rem(away * pow(STRIDE, -1, bins), bins)
    return owner, turn * cap + rank


def line_of(ids_ref):
    return jnp.concatenate([ids_ref[r:r + 1, :] for r in range(ids_ref.shape[0])], 1)


def scatter_kernel(bins, cap, emb_hbm, ids_ref, inbox, pinbox, counts, outbox, mine, emb_ref,
                   cnt_send, cnt_recv, send, recv, fwd_send, fwd_recv, loc):
    z, me = lax.axis_index("dp"), lax.axis_index("bin")
    sib = me + 1 - 2 * lax.rem(me, 2)
    jets = emb_hbm.shape[0]
    fetch = pltpu.make_async_copy(emb_hbm, emb_ref, loc.at[0])
    fetch.start()
    barrier = pltpu.get_barrier_semaphore()
    for k in range(1, bins):
        pl.semaphore_signal(barrier, inc=1, device_id=(z, lax.rem(me + k, bins)), device_id_type=MESH)
    owner, place = slot_places(line_of(ids_ref), me, bins, cap)
    hot = jnp.where(owner == iota((128, jets), 0), 1.0, 0.0).astype(BF16)
    tally = lax.dot_general(jnp.ones((8, jets), BF16), hot, NT, preferred_element_type=F32)
    mine[...] = tally[0:1, :].astype(jnp.int32)
    counts[me] = tally[0:1, :].astype(jnp.int32)
    pl.semaphore_wait(barrier, bins - 1)

    def count_copy(k):
        return pltpu.make_async_remote_copy(
            src_ref=mine, dst_ref=counts.at[me], send_sem=cnt_send.at[k], recv_sem=cnt_recv.at[k],
            device_id=(z, lax.rem(me + STRIDE * k, bins)), device_id_type=MESH)

    def row_copy(k):
        return pltpu.make_async_remote_copy(
            src_ref=outbox.at[k], dst_ref=inbox.at[me], send_sem=send.at[k], recv_sem=recv.at[k],
            device_id=(z, lax.rem(me + STRIDE * k, bins)), device_id_type=MESH)

    for k in range(1, bins):
        count_copy(k).start()
    group = 8 if bins % 8 == 0 else bins
    fetch.wait()
    emb = emb_ref[...]
    for first in range(0, bins, group):
        rows = group * cap
        pick = jnp.where(iota((rows, jets), 0) + first * cap == place, 1.0, 0.0).astype(BF16)
        block = jnp.dot(pick, emb, preferred_element_type=F32).astype(BF16)
        outbox[first:first + group] = block.reshape(group, cap, block.shape[1])
        for k in range(first, first + group):
            if k:
                row_copy(k).start()
    own = pltpu.make_async_copy(outbox.at[0], inbox.at[me], loc.at[1])
    own.start()

    def forward(src):
        return pltpu.make_async_remote_copy(
            src_ref=inbox.at[src], dst_ref=pinbox.at[src], send_sem=fwd_send, recv_sem=fwd_recv,
            device_id=(z, sib), device_id_type=MESH)

    own.wait()
    forward(me).start()
    for k in range(1, bins):
        row_copy(k).wait_recv()
        forward(lax.rem(me + STRIDE * (bins - k), bins)).start()
    for k in range(1, bins):
        count_copy(k).wait()
        row_copy(k).wait_send()
    pltpu.make_async_remote_copy(
        src_ref=inbox, dst_ref=pinbox, send_sem=fwd_send, recv_sem=fwd_recv,
        device_id=(z, sib), device_id_type=MESH).wait()


def pair_kernel(bins, cap, big, cnt_ref, spread_hbm, proj_ref, mine_ref, other_ref, out_ref, w_ref,
                spread_ref, loc, xs, ys, gs, fx, fy, sax, srx, sry, inner, gram, acc, rsum, tot):
    me = lax.axis_index("bin")
    width = proj_ref.shape[0]
    hw = width // 2
    sub = big // 2
    fetch = pltpu.make_async_copy(spread_hbm, spread_ref, loc)
    fetch.start()
    sib = me + 1 - 2 * lax.rem(me, 2)

    def pack(src_ref, dst, column):
        off = 0
        for s in range(bins):
            rows = src_ref[s].astype(F32)
            dst[0, pl.ds(off, cap), :] = rows[:, :hw]
            dst[1, pl.ds(off, cap), :] = rows[:, hw:]
            off = off + cnt_ref[s, 0, column]
        return off

    n_own = pack(mine_ref, xs, me)
    n_oth = pack(other_ref, ys, sib)
    for h in range(2):
        xs[h, pl.ds(n_own, big), :] = jnp.zeros((big, hw), F32)
    proj = proj_ref[...]
    ones = jnp.ones((8, width), BF16)
    subs_own = (n_own + sub - 1) // sub
    subs = (jnp.maximum(n_own, n_oth) + sub - 1) // sub

    def features(rows_ref, feat, col_sq, row_sq, n):
        def body(i, carry):
            base = pl.multiple_of(i * sub, sub)
            emb = jnp.concatenate([rows_ref[0, pl.ds(base, sub), :], rows_ref[1, pl.ds(base, sub), :]], 1)
            emb = jnp.where(iota((sub, width), 0) + base < n, emb, 0.0).astype(BF16)
            val = jnp.dot(emb, proj, preferred_element_type=F32).astype(BF16)
            feat[pl.ds(base, sub), :] = val
            sq = jnp.square(val.astype(F32))
            high = sq.astype(BF16)
            low = (sq - high.astype(F32)).astype(BF16)
            line = lax.dot_general(ones, high, NT, preferred_element_type=F32)
            line = line + lax.dot_general(ones, low, NT, preferred_element_type=F32)
            row_sq[i] = jnp.where(iota((8, sub), 1) + base < n, line, FAR)
            if col_sq is not None:
                col = jnp.broadcast_to(jnp.sum(sq, 1, keepdims=True), (sub, 128))
                col_sq[pl.ds(base, sub), :] = jnp.where(iota((sub, 128), 0) + base < n, col, FAR)
            return carry
        lax.fori_loop(0, subs, body, 0)

    features(xs, fx, sax, srx, n_own)
    features(ys, fy, None, sry, n_oth)

    fetch.wait()
    coef = [1.0 / jnp.full((8, 128), spread_ref[s], F32) / width for s in range(3)]
    rate = [c * math.log2(math.e) for c in coef]
    na = jnp.full((1, 128), jnp.maximum(n_own, 1).astype(F32), F32)
    nc = jnp.full((1, 128), jnp.maximum(n_oth, 1).astype(F32), F32)
    scale = float(bins * cap // 2 * width)
    k_self = jnp.concatenate([scale * (-(4.0 / (na * na)))] * 2, 1)
    k_cross = jnp.concatenate([scale * (4.0 / (na * nc))] * 2, 1)

    tot[...] = jnp.zeros_like(tot)
    w_ref[...] = jnp.zeros_like(w_ref)

    feats = (fx, fy)
    row_sqs = (srx, sry)

    def meet(which, rows, cols, base, col):
        xa = fx[pl.ds(base, rows), :]
        xb = feats[which][pl.ds(pl.multiple_of(col * sub, sub), cols), :]
        inner[which, 0:rows, 0:cols] = lax.dot_general(xa + xa, xb, NT, preferred_element_type=F32)

    def weigh(which, rows, cols, base, col):
        for p in range(0, cols, 128):
            sb = row_sqs[which][col + p // 128]
            total = jnp.zeros((8, 128), F32)
            for r in range(0, rows, 16):
                parts = []
                for q in (r, r + 8):
                    t = inner[which, q:q + 8, p:p + 128] - sax[pl.ds(base + q, 8), :] - sb
                    e0 = jnp.exp2(t * rate[0])
                    e1 = jnp.exp2(t * rate[1])
                    e2 = jnp.exp2(t * rate[2])
                    total = total + (e0 + e1 + e2)
                    parts.append(e0 * coef[0] + e1 * coef[1] + e2 * coef[2])
                gram[which, r:r + 16, p:p + 128] = jnp.concatenate(parts, 0).astype(BF16)
            tot[which] += total

    def pull(which, rows, cols, col):
        xb = feats[which][pl.ds(pl.multiple_of(col * sub, sub), cols), :]
        g = gram[which, 0:rows, 0:cols]
        acc[which, 0:rows, :] += jnp.dot(g, xb, preferred_element_type=F32)
        rsum[which, 0:rows, :] += jnp.dot(g, jnp.ones((cols, 128), BF16), preferred_element_type=F32)

    def row_block(rows, base):
        acc[:, 0:rows, :] = jnp.zeros((2, rows, width), F32)
        rsum[:, 0:rows, :] = jnp.zeros((2, rows, 128), F32)
        blocks = subs // 2

        @pl.when(blocks > 0)
        def _():
            gram[1, 0:rows, :] = jnp.zeros((rows, big), BF16)
            meet(0, rows, big, base, 0)

            def body(j, carry):
                meet(1, rows, big, base, 2 * j)
                pull(1, rows, big, 2 * jnp.maximum(j - 1, 0))
                weigh(0, rows, big, base, 2 * j)
                meet(0, rows, big, base, 2 * jnp.minimum(j + 1, blocks - 1))
                pull(0, rows, big, 2 * j)
                weigh(1, rows, big, base, 2 * j)
                return carry
            lax.fori_loop(0, blocks, body, 0)
            pull(1, rows, big, 2 * (blocks - 1))

        @pl.when(subs % 2 == 1)
        def _():
            for which in (0, 1):
                meet(which, rows, sub, base, subs - 1)
            for which in (0, 1):
                weigh(which, rows, sub, base, subs - 1)
                pull(which, rows, sub, subs - 1)

        xf = fx[pl.ds(base, rows), :].astype(F32)
        force = [xf * jnp.concatenate([rsum[which, 0:rows, :]] * 2, 1) - acc[which, 0:rows, :] for which in (0, 1)]
        gz = (k_self * force[0] + k_cross * force[1]).astype(BF16)
        ge = lax.dot_general(gz, proj, NT, preferred_element_type=F32)
        gs[0, pl.ds(base, rows), :] = ge[:, :hw]
        gs[1, pl.ds(base, rows), :] = ge[:, hw:]
        emb = jnp.concatenate([xs[0, pl.ds(base, rows), :], xs[1, pl.ds(base, rows), :]], 1).astype(BF16)
        gw = lax.dot_general(emb, gz, TN, preferred_element_type=F32)
        w_ref[0, :width, :] += gw[:, :hw]
        w_ref[1, :width, :] += gw[:, hw:]

    def full(i, carry):
        row_block(big, pl.multiple_of(i * big, big))
        return carry
    lax.fori_loop(0, subs_own // 2, full, 0)

    @pl.when(subs_own % 2 == 1)
    def _():
        row_block(sub, pl.multiple_of((subs_own - 1) * sub, sub))

    for h in range(2):
        gs[h, pl.ds(n_own, cap), :] = jnp.zeros((cap, hw), F32)
    share = jnp.sum(tot[0], 0, keepdims=True) / (na * na) - jnp.sum(tot[1], 0, keepdims=True) / (na * nc)
    for h in range(2):
        w_ref[h, width:width + 8, :] = jnp.broadcast_to(share, (8, 128))
    off = 0
    for s in range(bins):
        out_ref[s, :, :hw] = gs[0, pl.ds(off, cap), :].astype(BF16)
        out_ref[s, :, hw:] = gs[1, pl.ds(off, cap), :].astype(BF16)
        off = off + cnt_ref[s, 0, me]


def return_kernel(bins, reps, cap, slots, w_ref, ids_ref, g_out, w_out, l_out,
                  inbox, pick, p_recv, z_send, z_recv, plane, zg, other,
                  send, recv, psem, zsem, asem, zgsem, fsem, loc):
    z, me = lax.axis_index("dp"), lax.axis_index("bin")
    core = lax.rem(me, 2)
    q = lax.div(me, 2)
    chips = bins // 2
    sib = me + 1 - 2 * core
    jets = g_out.shape[0]
    width = g_out.shape[1]
    zr = width // reps
    barrier = pltpu.get_barrier_semaphore()
    for k in range(1, bins):
        pl.semaphore_signal(barrier, inc=1, device_id=(z, lax.rem(me + k, bins)), device_id_type=MESH)
    for k in range(1, reps):
        pl.semaphore_signal(barrier, inc=1, device_id=(lax.rem(z + k, reps), me), device_id_type=MESH)
    pl.semaphore_wait(barrier, bins - 1 + reps - 1)

    def remote(src, dst, ssem, rsem, dev):
        return pltpu.make_async_remote_copy(
            src_ref=src, dst_ref=dst, send_sem=ssem, recv_sem=rsem, device_id=dev, device_id_type=MESH)

    pair = remote(w_ref.at[1 - core], p_recv, psem.at[0], psem.at[1], (z, sib))
    pair.start()

    def row_copy(k):
        dest = lax.rem(me + STRIDE * k, bins)
        return remote(slots.at[dest], inbox.at[bins - k], send, recv, (z, dest))

    for k in range(1, bins):
        row_copy(k).start()
    own = pltpu.make_async_copy(slots.at[me], inbox.at[0], loc)
    own.start()

    _, place = slot_places(line_of(ids_ref), me, bins, cap)

    pair.wait()
    loss_tile = w_ref[core, width:width + 8, :] + p_recv[width:width + 8, :]
    for k in range(reps):
        z_send[k, 0:zr, :] = w_ref[core, k * zr:(k + 1) * zr, :] + p_recv[k * zr:(k + 1) * zr, :]
        z_send[k, zr:zr + 8, :] = loss_tile

    def z_copy(k):
        dest = lax.rem(z + k, reps)
        return remote(z_send.at[dest], z_recv.at[z], zsem.at[0, k], zsem.at[1, k], (dest, me))

    for k in range(1, reps):
        z_copy(k).start()
    z_recv[z] = z_send[z]

    for first in range(0, jets, 128 if jets % 128 == 0 else jets):
        size = min(128, jets - first)
        part = jnp.broadcast_to(place[:, first:first + size], (size, size))
        column = jnp.sum(jnp.where(iota((size, size), 0) == iota((size, size), 1), part, 0), 1, keepdims=True)
        pick[first:first + size, :] = jnp.where(column == iota((size, bins * cap), 1), 1.0, 0.0).astype(BF16)

    for k in range(1, reps):
        z_copy(k).wait()
    chunk = z_recv[0]
    for k in range(1, reps):
        chunk = chunk + z_recv[k]
    plane[q] = chunk

    def plane_copy(k):
        dest = lax.rem(q + k, chips)
        return remote(plane.at[q], plane.at[q], asem.at[0, k], asem.at[1, k], (z, 2 * dest + core))

    for k in range(1, chips):
        plane_copy(k).start()

    own.wait()
    remote(slots.at[pl.ds(0, bins - 1)], inbox.at[pl.ds(1, bins - 1)], send, recv, (z, sib)).wait()
    g_out[...] = jnp.dot(pick[...], inbox[...].reshape(bins * cap, width), preferred_element_type=F32).astype(BF16)

    for k in range(1, chips):
        plane_copy(k).wait()
    whole = plane[0]
    for k in range(1, chips):
        whole = whole + plane[k]
    l_out[...] = jnp.broadcast_to(jnp.sum(whole[zr:zr + 1, :], 1, keepdims=True) / reps, (1, 128))
    zg[z] = whole[0:zr, :]

    def zg_copy(k):
        dest = lax.rem(z + k, reps)
        return remote(zg.at[z], zg.at[z], zgsem.at[0, k], zgsem.at[1, k], (dest, me))

    def hand_over(at):
        return remote(zg.at[at], other.at[at], fsem.at[0], fsem.at[1], (z, sib))

    for k in range(1, reps):
        zg_copy(k).start()
    hand_over(z).start()
    for k in range(1, reps):
        zg_copy(k).wait_recv()
        hand_over(lax.rem(z + reps - k, reps)).start()
    for k in range(1, reps):
        zg_copy(k).wait_send()
    remote(zg, other, fsem.at[0], fsem.at[1], (z, sib)).wait()
    tokens = float(jets * bins * reps)
    here = zg[...].reshape(width, 128) / tokens
    there = other[...].reshape(width, 128) / tokens
    w_out[:, 0:128] = jnp.where(core == 0, here, there)
    w_out[:, 128:256] = jnp.where(core == 0, there, here)


def vmem(count):
    return [pl.BlockSpec(memory_space=pltpu.VMEM)] * count


def local(embeddings, bin_ids, spreads, projection):
    jets, width = embeddings.shape
    bins, reps = lax.axis_size("bin"), lax.axis_size("dp")
    cap = 2 * jets // bins
    most = bins * cap
    chips = bins // 2
    ids = bin_ids.reshape(-1, 128) if jets % 128 == 0 else bin_ids.reshape(1, jets)
    dma = pltpu.SemaphoreType.DMA
    box = jax.ShapeDtypeStruct((bins, cap, width), BF16)
    limit = 48 << 20
    inbox, pinbox, counts = pl.pallas_call(
        functools.partial(scatter_kernel, bins, cap),
        out_shape=(box, box, jax.ShapeDtypeStruct((bins, 1, 128), jnp.int32)),
        in_specs=[pl.BlockSpec(memory_space=pltpu.HBM)] + vmem(1), out_specs=tuple(vmem(3)),
        scratch_shapes=[
            pltpu.VMEM((bins, cap, width), BF16), pltpu.VMEM((1, 128), jnp.int32), pltpu.VMEM((jets, width), BF16),
            dma((bins,)), dma((bins,)), dma((bins,)), dma((bins,)), dma, dma, dma((2,))],
        compiler_params=pltpu.CompilerParams(collective_id=0, has_side_effects=True, vmem_limit_bytes=limit),
        name="scatter",
    )(embeddings, ids)

    big = 256
    top = -(-most // big) * big
    room = top + big
    slots, w_part = pl.pallas_call(
        functools.partial(pair_kernel, bins, cap, big),
        out_shape=(box, jax.ShapeDtypeStruct((2, width + 8, 128), F32)),
        in_specs=[pl.BlockSpec(memory_space=pltpu.SMEM), pl.BlockSpec(memory_space=pltpu.HBM)] + vmem(3),
        out_specs=tuple(vmem(2)),
        scratch_shapes=[
            pltpu.SMEM((3,), F32), dma,
            pltpu.VMEM((2, room, width // 2), F32), pltpu.VMEM((2, room, width // 2), F32),
            pltpu.VMEM((2, room, width // 2), F32),
            pltpu.VMEM((top, width), BF16), pltpu.VMEM((top, width), BF16), pltpu.VMEM((top, 128), F32),
            pltpu.VMEM((2 * top // big, 8, big // 2), F32), pltpu.VMEM((2 * top // big, 8, big // 2), F32),
            pltpu.VMEM((2, big, big), F32), pltpu.VMEM((2, big, big), BF16),
            pltpu.VMEM((2, big, width), F32), pltpu.VMEM((2, big, 128), F32), pltpu.VMEM((2, 8, 128), F32)],
        compiler_params=pltpu.CompilerParams(vmem_limit_bytes=limit),
        name="pairs",
    )(counts, spreads, projection, inbox, pinbox)

    zr = width // reps
    grad_emb, grad_w, loss = pl.pallas_call(
        functools.partial(return_kernel, bins, reps, cap),
        out_shape=(jax.ShapeDtypeStruct((jets, width), BF16), jax.ShapeDtypeStruct((width, width), F32),
                   jax.ShapeDtypeStruct((1, 128), F32)),
        in_specs=vmem(3), out_specs=tuple(vmem(3)),
        scratch_shapes=[
            pltpu.VMEM((bins, cap, width), BF16), pltpu.VMEM((jets, most), BF16),
            pltpu.VMEM((width + 8, 128), F32),
            pltpu.VMEM((reps, zr + 8, 128), F32), pltpu.VMEM((reps, zr + 8, 128), F32),
            pltpu.VMEM((chips, zr + 8, 128), F32), pltpu.VMEM((reps, zr, 128), F32), pltpu.VMEM((reps, zr, 128), F32),
            dma, dma, dma((2,)), dma((2, reps)), dma((2, chips)), dma((2, reps)), dma((2,)), dma],
        compiler_params=pltpu.CompilerParams(collective_id=1, has_side_effects=True, vmem_limit_bytes=limit),
        name="giveback",
    )(slots, w_part, ids)
    return grad_emb, grad_w, loss[0, 0]


def solution(mesh):
    return jax.shard_map(
        local,
        mesh=mesh,
        in_specs=(P(("dp", "bin"), None), P(("dp", "bin")), P(), P()),
        out_specs=(P(("dp", "bin"), None), P(), P()),
        check_vma=False,
    )
```

```python
import functools
import math

import jax
import jax.numpy as jnp
from jax import lax
from jax.experimental import pallas as pl
from jax.experimental.pallas import tpu as pltpu
from jax.sharding import PartitionSpec as P

MESH = pl.DeviceIdType.MESH
F32 = jnp.float32
BF16 = jnp.bfloat16
FAR = 1e30
EMPTY = 1024.0
NT = (((1,), (1,)), ((), ()))
TN = (((0,), (0,)), ((), ()))


def iota(shape, dim):
    return lax.broadcasted_iota(jnp.int32, shape, dim)


def grid_of(bins):
    chips = bins // 2
    nx = max(d for d in range(1, chips + 1) if chips % d == 0 and d * d <= chips)
    return nx, chips // nx


def hops(step, size):
    return min(step, size - step)


def plane_steps(bins):
    nx, ny = grid_of(bins)
    steps = [(dx, dy) for dx in range(nx) for dy in range(ny)]
    return sorted(steps, key=lambda d: -(hops(d[0], nx) + hops(d[1], ny)))


def turns(bins):
    ny = grid_of(bins)[1]
    codes = [2 * (dx * ny + dy) + dc for dx, dy in plane_steps(bins) for dc in range(2)]
    return [code for code in codes if code]


def back(code, bins):
    nx, ny = grid_of(bins)
    dx, dy, dc = code // (2 * ny), code // 2 % ny, code % 2
    return 2 * ((-dx % nx) * ny + -dy % ny) + dc


def chip_at(q, dx, dy, bins):
    nx, ny = grid_of(bins)
    return lax.rem(lax.div(q, ny) + dx, nx) * ny + lax.rem(lax.rem(q, ny) + dy, ny)


def device_at(me, code, bins):
    ny = grid_of(bins)[1]
    chip = chip_at(lax.div(me, 2), code // (2 * ny), code // 2 % ny, bins)
    return 2 * chip + lax.rem(lax.rem(me, 2) + code % 2, 2)


def slot_places(ids, me, bins, cap):
    nx, ny = grid_of(bins)
    half = bins // 2
    jets = ids.shape[1]
    upper = ids >= half
    chip = jnp.where(upper, ids - half, ids)
    dx = chip // ny - lax.div(me, 2 * ny)
    dx = jnp.where(dx < 0, dx + nx, dx)
    dy = chip % ny - lax.rem(lax.div(me, 2), ny)
    dy = jnp.where(dy < 0, dy + ny, dy)
    dc = jnp.where(upper, 1, 0) - lax.rem(me, 2)
    code = 2 * (dx * ny + dy) + jnp.where(dc < 0, 1, dc)
    step = 256 if jets % 256 == 0 else jets
    before = jnp.where(iota((step, step), 0) < iota((step, step), 1), 1.0, 0.0).astype(BF16)
    wide = max(bins, 16)
    carry = jnp.zeros((wide, 1), F32)
    ranks = []
    for start in range(0, jets, step):
        hot = jnp.where(code[:, start:start + step] == iota((wide, step), 0), 1.0, 0.0)
        seen = jnp.dot(hot.astype(BF16), before, preferred_element_type=F32) + carry
        ranks.append(jnp.sum(seen * hot, 0, keepdims=True))
        carry = carry + jnp.sum(hot, 1, keepdims=True)
    rank = jnp.concatenate(ranks, 1).astype(jnp.int32)
    return code * cap + rank


def line_of(ids_ref):
    return jnp.concatenate([ids_ref[r:r + 1, :] for r in range(ids_ref.shape[0])], 1)


def scatter_kernel(bins, cap, emb_hbm, ids_hbm, inbox, pinbox, counts, pcounts, outbox, emb_ref, ids_ref,
                   send, recv, fwd_send, fwd_recv, cnt_sem, loc):
    z, me = lax.axis_index("dp"), lax.axis_index("bin")
    sib = me + 1 - 2 * lax.rem(me, 2)
    jets = emb_hbm.shape[0]
    fetch_ids = pltpu.make_async_copy(ids_hbm, ids_ref, loc.at[1])
    fetch_ids.start()
    fetch = pltpu.make_async_copy(emb_hbm, emb_ref, loc.at[0])
    fetch.start()
    barrier = pltpu.get_barrier_semaphore()
    for k in range(1, bins):
        pl.semaphore_signal(barrier, inc=1, device_id=(z, lax.rem(me + k, bins)), device_id_type=MESH)
    fetch_ids.wait()
    place = slot_places(line_of(ids_ref), me, bins, cap)

    def row_copy(k):
        return pltpu.make_async_remote_copy(
            src_ref=outbox.at[k], dst_ref=inbox.at[me], send_sem=send, recv_sem=recv.at[k],
            device_id=(z, device_at(me, k, bins)), device_id_type=MESH)

    group = 8 if bins % 8 == 0 else bins
    fetch.wait()
    emb = emb_ref[...]
    solid = jnp.ones((jets, 128), BF16)
    for first in range(0, bins, group):
        rows = group * cap
        pick = jnp.where(iota((rows, jets), 0) + first * cap == place, 1.0, 0.0).astype(BF16)
        block = jnp.dot(pick, emb, preferred_element_type=F32)
        taken = jnp.dot(pick, solid, preferred_element_type=F32)
        outbox[first:first + group, :, 0:128] = jnp.where(
            taken > 0.5, block[:, 0:128], EMPTY).astype(BF16).reshape(group, cap, 128)
        outbox[first:first + group, :, 128:256] = block[:, 128:256].astype(BF16).reshape(group, cap, 128)
    pl.semaphore_wait(barrier, bins - 1)
    for k in turns(bins):
        row_copy(k).start()
    own = pltpu.make_async_copy(outbox.at[0], inbox.at[me], loc.at[1])
    own.start()

    def forward(src):
        return pltpu.make_async_remote_copy(
            src_ref=inbox.at[src], dst_ref=pinbox.at[src], send_sem=fwd_send, recv_sem=fwd_recv,
            device_id=(z, sib), device_id_type=MESH)

    def tally(src):
        live = jnp.where(inbox[src, :, 0:128].astype(F32) < EMPTY / 2, 1.0, 0.0)
        return jnp.where(iota((1, 128), 1) == src, jnp.sum(live, 0, keepdims=True), 0.0)

    own.wait()
    forward(me).start()
    table = tally(me)
    for k in turns(bins):
        row_copy(k).wait_recv()
        src = device_at(me, back(k, bins), bins)
        forward(src).start()
        table = table + tally(src)
    counts[...] = table.astype(jnp.int32)
    swap = pltpu.make_async_remote_copy(
        src_ref=counts, dst_ref=pcounts, send_sem=cnt_sem.at[0], recv_sem=cnt_sem.at[1],
        device_id=(z, sib), device_id_type=MESH)
    swap.start()
    pltpu.make_async_remote_copy(
        src_ref=outbox.at[pl.ds(1, bins - 1)], dst_ref=inbox.at[pl.ds(1, bins - 1)], send_sem=send, recv_sem=fwd_recv,
        device_id=(z, sib), device_id_type=MESH).wait_send()
    swap.wait()
    pltpu.make_async_remote_copy(
        src_ref=inbox, dst_ref=pinbox, send_sem=fwd_send, recv_sem=fwd_recv,
        device_id=(z, sib), device_id_type=MESH).wait()


def pair_kernel(bins, cap, big, cnt_ref, pcnt_ref, spread_hbm, proj_ref, mine_ref, other_ref, out_ref, w_ref,
                spread_ref, loc, xs, ys, gs, fx, fy, sax, srx, sry, inner, gram, acc, rsum, tot):
    width = proj_ref.shape[0]
    hw = width // 2
    sub = big // 2
    fetch = pltpu.make_async_copy(spread_hbm, spread_ref, loc)
    fetch.start()

    def pack(src_ref, dst, cnt):
        off = 0
        for s in range(bins):
            rows = src_ref[s].astype(F32)
            dst[0, pl.ds(off, cap), :] = rows[:, :hw]
            dst[1, pl.ds(off, cap), :] = rows[:, hw:]
            off = off + cnt[0, s]
        return off

    n_own = pack(mine_ref, xs, cnt_ref)
    n_oth = pack(other_ref, ys, pcnt_ref)
    for h in range(2):
        xs[h, pl.ds(n_own, big), :] = jnp.zeros((big, hw), F32)
    proj = proj_ref[...]
    ones = jnp.ones((8, width), BF16)
    subs_own = (n_own + sub - 1) // sub
    subs = (jnp.maximum(n_own, n_oth) + sub - 1) // sub

    def features(i, carry):
        base = pl.multiple_of(i * big, big)
        for rows_ref, feat, col_sq, row_sq, n in ((xs, fx, sax, srx, n_own), (ys, fy, None, sry, n_oth)):
            emb = jnp.concatenate([rows_ref[0, pl.ds(base, big), :], rows_ref[1, pl.ds(base, big), :]], 1)
            emb = jnp.where(iota((big, width), 0) + base < n, emb, 0.0).astype(BF16)
            val = jnp.dot(emb, proj, preferred_element_type=F32).astype(BF16)
            feat[pl.ds(base, big), :] = val
            sq = jnp.square(val.astype(F32))
            high = sq.astype(BF16)
            low = (sq - high.astype(F32)).astype(BF16)
            line = lax.dot_general(ones, high, NT, preferred_element_type=F32)
            line = line + lax.dot_general(ones, low, NT, preferred_element_type=F32)
            line = jnp.where(iota((8, big), 1) + base < n, line, FAR)
            row_sq[2 * i] = line[:, 0:sub]
            row_sq[2 * i + 1] = line[:, sub:big]
            if col_sq is not None:
                col = jnp.broadcast_to(jnp.sum(sq, 1, keepdims=True), (big, 128))
                col_sq[pl.ds(base, big), :] = jnp.where(iota((big, 128), 0) + base < n, col, FAR)
        return carry
    lax.fori_loop(0, (subs + 1) // 2, features, 0)

    fetch.wait()
    coef = [1.0 / jnp.full((8, 128), spread_ref[s], F32) / width for s in range(3)]
    rate = [c * math.log2(math.e) for c in coef]
    na = jnp.full((1, 128), jnp.maximum(n_own, 1).astype(F32), F32)
    nc = jnp.full((1, 128), jnp.maximum(n_oth, 1).astype(F32), F32)
    scale = float(bins * cap // 2 * width)
    k_self = jnp.concatenate([scale * (-(4.0 / (na * na)))] * 2, 1)
    k_cross = jnp.concatenate([scale * (4.0 / (na * nc))] * 2, 1)

    tot[...] = jnp.zeros_like(tot)
    w_ref[...] = jnp.zeros_like(w_ref)

    feats = (fx, fy)
    row_sqs = (srx, sry)

    def meet(which, rows, cols, base, col, at=0):
        xa = fx[pl.ds(base, rows), :]
        xb = feats[which][pl.ds(pl.multiple_of(col * sub, sub) + at, cols), :]
        inner[which, 0:rows, at:at + cols] = lax.dot_general(xa + xa, xb, NT, preferred_element_type=F32)

    def weigh(which, rows, cols, base, col, beside=()):
        steps = [(p, r) for p in range(0, cols, 128) for r in range(0, rows, 16)]
        beside = list(beside)
        every = max(1, len(steps) // (len(beside) + 1))
        total = jnp.zeros((8, 128), F32)
        for at, (p, r) in enumerate(steps):
            if beside and at % every == 0:
                beside.pop(0)()
            sb = row_sqs[which][col + p // sub, :, p % sub:p % sub + 128]
            parts = []
            for q in (r, r + 8):
                t = inner[which, q:q + 8, p:p + 128] - sax[pl.ds(base + q, 8), :] - sb
                e0 = jnp.exp2(t * rate[0])
                e1 = jnp.exp2(t * rate[1])
                e2 = jnp.exp2(t * rate[2])
                total = total + (e0 + e1 + e2)
                parts.append(e0 * coef[0] + e1 * coef[1] + e2 * coef[2])
            gram[which, r:r + 16, p:p + 128] = jnp.concatenate(parts, 0).astype(BF16)
        tot[which] += total
        for rest in beside:
            rest()

    def pull(which, rows, cols, col):
        xb = feats[which][pl.ds(pl.multiple_of(col * sub, sub), cols), :]
        acc[which, 0:rows, :] += jnp.dot(gram[which, 0:rows, 0:cols], xb, preferred_element_type=F32)

    def count(which, rows, cols):
        rsum[which, 0:rows, :] += jnp.dot(
            gram[which, 0:rows, 0:cols], jnp.ones((cols, 128), BF16), preferred_element_type=F32)

    def row_block(rows, base):
        acc[:, 0:rows, :] = jnp.zeros((2, rows, width), F32)
        rsum[:, 0:rows, :] = jnp.zeros((2, rows, 128), F32)
        blocks = subs // 2

        @pl.when(blocks > 0)
        def _():
            gram[1, 0:rows, :] = jnp.zeros((rows, big), BF16)
            meet(0, rows, big, base, 0)

            def turn(which, j, prev, later):
                other = 1 - which
                weigh(which, rows, big, base, 2 * j, [
                    lambda: meet(other, rows, sub, base, later, 0),
                    lambda: meet(other, rows, sub, base, later, sub),
                    lambda: pull(other, rows, big, prev),
                    lambda: count(other, rows, big)])

            def body(j, carry):
                turn(0, j, 2 * jnp.maximum(j - 1, 0), 2 * j)
                turn(1, j, 2 * j, 2 * jnp.minimum(j + 1, blocks - 1))
                return carry
            lax.fori_loop(0, blocks, body, 0)
            pull(1, rows, big, 2 * (blocks - 1))
            count(1, rows, big)

        @pl.when(subs % 2 == 1)
        def _():
            for which in (0, 1):
                meet(which, rows, sub, base, subs - 1)
            for which in (0, 1):
                weigh(which, rows, sub, base, subs - 1)
                pull(which, rows, sub, subs - 1)
                count(which, rows, sub)

        xf = fx[pl.ds(base, rows), :].astype(F32)
        force = [xf * jnp.concatenate([rsum[which, 0:rows, :]] * 2, 1) - acc[which, 0:rows, :] for which in (0, 1)]
        gz = (k_self * force[0] + k_cross * force[1]).astype(BF16)
        ge = lax.dot_general(gz, proj, NT, preferred_element_type=F32)
        gs[0, pl.ds(base, rows), :] = ge[:, :hw]
        gs[1, pl.ds(base, rows), :] = ge[:, hw:]
        emb = jnp.concatenate([xs[0, pl.ds(base, rows), :], xs[1, pl.ds(base, rows), :]], 1).astype(BF16)
        gw = lax.dot_general(emb, gz, TN, preferred_element_type=F32)
        w_ref[0, :width, :] += gw[:, :hw]
        w_ref[1, :width, :] += gw[:, hw:]

    def full(i, carry):
        row_block(big, pl.multiple_of(i * big, big))
        return carry
    lax.fori_loop(0, subs_own // 2, full, 0)

    @pl.when(subs_own % 2 == 1)
    def _():
        row_block(sub, pl.multiple_of((subs_own - 1) * sub, sub))

    for h in range(2):
        gs[h, pl.ds(n_own, cap), :] = jnp.zeros((cap, hw), F32)
    share = jnp.sum(tot[0], 0, keepdims=True) / (na * na) - jnp.sum(tot[1], 0, keepdims=True) / (na * nc)
    for h in range(2):
        w_ref[h, width:width + 8, :] = jnp.broadcast_to(share, (8, 128))
    off = 0
    for s in range(bins):
        out_ref[s, :, :hw] = gs[0, pl.ds(off, cap), :].astype(BF16)
        out_ref[s, :, hw:] = gs[1, pl.ds(off, cap), :].astype(BF16)
        off = off + cnt_ref[0, s]


def return_kernel(bins, reps, cap, slots, w_ref, ids_ref, g_out, w_out, l_out,
                  inbox, pick, p_recv, a_send, a_recv, zx, full, other,
                  send, recv, psem, asem, zsem, gsem, fsem, loc):
    z, me = lax.axis_index("dp"), lax.axis_index("bin")
    core = lax.rem(me, 2)
    q = lax.div(me, 2)
    chips = bins // 2
    sib = me + 1 - 2 * core
    jets = g_out.shape[0]
    width = g_out.shape[1]
    ar = width // chips
    tokens = float(jets * bins * reps)
    barrier = pltpu.get_barrier_semaphore()
    for k in range(1, bins):
        pl.semaphore_signal(barrier, inc=1, device_id=(z, lax.rem(me + k, bins)), device_id_type=MESH)
    for k in range(1, reps):
        pl.semaphore_signal(barrier, inc=1, device_id=(lax.rem(z + k, reps), me), device_id_type=MESH)

    place = slot_places(line_of(ids_ref), me, bins, cap)
    for first in range(0, jets, 128 if jets % 128 == 0 else jets):
        size = min(128, jets - first)
        part = jnp.broadcast_to(place[:, first:first + size], (size, size))
        column = jnp.sum(jnp.where(iota((size, size), 0) == iota((size, size), 1), part, 0), 1, keepdims=True)
        pick[first:first + size, :] = jnp.where(column == iota((size, bins * cap), 1), 1.0, 0.0).astype(BF16)
    pl.semaphore_wait(barrier, bins - 1 + reps - 1)

    def remote(src, dst, sems, dev):
        return pltpu.make_async_remote_copy(
            src_ref=src, dst_ref=dst, send_sem=sems.at[0], recv_sem=sems.at[1], device_id=dev, device_id_type=MESH)

    pair = remote(w_ref.at[1 - core], p_recv, psem, (z, sib))
    pair.start()

    def row_copy(k):
        dest = device_at(me, k, bins)
        return pltpu.make_async_remote_copy(
            src_ref=slots.at[dest], dst_ref=inbox.at[back(k, bins)], send_sem=send, recv_sem=recv,
            device_id=(z, dest), device_id_type=MESH)

    own = pltpu.make_async_copy(slots.at[me], inbox.at[0], loc)
    own.start()
    around = sorted(range(1, reps), key=lambda k: -hops(k, reps))

    pair.wait()
    loss_tile = w_ref[core, width:width + 8, :] + p_recv[width:width + 8, :]
    for k in range(chips):
        a_send[k, 0:ar, :] = w_ref[core, k * ar:(k + 1) * ar, :] + p_recv[k * ar:(k + 1) * ar, :]
        a_send[k, ar:ar + 8, :] = loss_tile

    others = [chip_at(q, dx, dy, bins) for dx, dy in plane_steps(bins) if dx or dy]
    for chip in others:
        remote(a_send.at[chip], a_recv.at[q], asem, (z, 2 * chip + core)).start()
    a_recv[q] = a_send[q]
    remote(a_send.at[pl.ds(0, chips - 1)], a_recv.at[pl.ds(0, chips - 1)], asem, (z, sib)).wait()
    for k in turns(bins):
        row_copy(k).start()
    chunk = a_recv[0]
    for k in range(1, chips):
        chunk = chunk + a_recv[k]
    zx[z] = chunk
    for k in around:
        remote(zx.at[z], zx.at[z], zsem, (lax.rem(z + k, reps), me)).start()
    remote(zx.at[pl.ds(0, reps - 1)], zx.at[pl.ds(0, reps - 1)], zsem, (z, sib)).wait()
    chunk = zx[0]
    for k in range(1, reps):
        chunk = chunk + zx[k]
    full[q] = chunk[0:ar, :] / tokens
    for chip in others:
        remote(full.at[q], full.at[q], gsem, (z, 2 * chip + core)).start()
    l_out[...] = jnp.broadcast_to(jnp.sum(chunk[ar:ar + 1, :], 1, keepdims=True) / reps, (1, 128))

    own.wait()
    pltpu.make_async_remote_copy(
        src_ref=slots.at[pl.ds(0, bins - 1)], dst_ref=inbox.at[pl.ds(1, bins - 1)], send_sem=send, recv_sem=recv,
        device_id=(z, sib), device_id_type=MESH).wait()
    g_out[...] = jnp.dot(pick[...], inbox[...].reshape(bins * cap, width), preferred_element_type=F32).astype(BF16)

    remote(full.at[pl.ds(0, chips - 1)], full.at[pl.ds(0, chips - 1)], gsem, (z, sib)).wait()
    last = remote(full, other, fsem, (z, sib))
    last.start()
    last.wait()
    here = full[...].reshape(width, 128)
    there = other[...].reshape(width, 128)
    w_out[:, 0:128] = jnp.where(core == 0, here, there)
    w_out[:, 128:256] = jnp.where(core == 0, there, here)


def vmem(count):
    return [pl.BlockSpec(memory_space=pltpu.VMEM)] * count


def local(embeddings, bin_ids, spreads, projection):
    jets, width = embeddings.shape
    bins, reps = lax.axis_size("bin"), lax.axis_size("dp")
    cap = 2 * jets // bins
    most = bins * cap
    chips = bins // 2
    ids = bin_ids.reshape(-1, 128) if jets % 128 == 0 else bin_ids.reshape(1, jets)
    dma = pltpu.SemaphoreType.DMA
    box = jax.ShapeDtypeStruct((bins, cap, width), BF16)
    limit = 48 << 20
    tally = jax.ShapeDtypeStruct((1, 128), jnp.int32)
    inbox, pinbox, counts, pcounts = pl.pallas_call(
        functools.partial(scatter_kernel, bins, cap),
        out_shape=(box, box, tally, tally),
        in_specs=[pl.BlockSpec(memory_space=pltpu.HBM)] * 2, out_specs=tuple(vmem(4)),
        scratch_shapes=[
            pltpu.VMEM((bins, cap, width), BF16), pltpu.VMEM((jets, width), BF16), pltpu.VMEM(ids.shape, jnp.int32),
            dma, dma((bins,)), dma, dma, dma((2,)), dma((2,))],
        compiler_params=pltpu.CompilerParams(collective_id=0, has_side_effects=True, vmem_limit_bytes=limit),
        name="scatter",
    )(embeddings, ids)

    big = 512
    top = -(-most // big) * big
    room = top + big
    slots, w_part = pl.pallas_call(
        functools.partial(pair_kernel, bins, cap, big),
        out_shape=(box, jax.ShapeDtypeStruct((2, width + 8, 128), F32)),
        in_specs=[pl.BlockSpec(memory_space=pltpu.SMEM)] * 2 + [pl.BlockSpec(memory_space=pltpu.HBM)] + vmem(3),
        out_specs=tuple(vmem(2)),
        scratch_shapes=[
            pltpu.SMEM((3,), F32), dma,
            pltpu.VMEM((2, room, width // 2), F32), pltpu.VMEM((2, room, width // 2), F32),
            pltpu.VMEM((2, room, width // 2), F32),
            pltpu.VMEM((top, width), BF16), pltpu.VMEM((top, width), BF16), pltpu.VMEM((top, 128), F32),
            pltpu.VMEM((2 * top // big, 8, big // 2), F32), pltpu.VMEM((2 * top // big, 8, big // 2), F32),
            pltpu.VMEM((2, big, big), F32), pltpu.VMEM((2, big, big), BF16),
            pltpu.VMEM((2, big, width), F32), pltpu.VMEM((2, big, 128), F32), pltpu.VMEM((2, 8, 128), F32)],
        compiler_params=pltpu.CompilerParams(vmem_limit_bytes=limit),
        name="pairs",
    )(counts, pcounts, spreads, projection, inbox, pinbox)

    ar = width // chips
    grad_emb, grad_w, loss = pl.pallas_call(
        functools.partial(return_kernel, bins, reps, cap),
        out_shape=(jax.ShapeDtypeStruct((jets, width), BF16), jax.ShapeDtypeStruct((width, width), F32),
                   jax.ShapeDtypeStruct((1, 128), F32)),
        in_specs=vmem(3), out_specs=tuple(vmem(3)),
        scratch_shapes=[
            pltpu.VMEM((bins, cap, width), BF16), pltpu.VMEM((jets, most), BF16),
            pltpu.VMEM((width + 8, 128), F32),
            pltpu.VMEM((chips, ar + 8, 128), F32), pltpu.VMEM((chips, ar + 8, 128), F32),
            pltpu.VMEM((reps, ar + 8, 128), F32), pltpu.VMEM((chips, ar, 128), F32), pltpu.VMEM((chips, ar, 128), F32),
            dma, dma, dma((2,)), dma((2,)), dma((2,)), dma((2,)), dma((2,)), dma],
        compiler_params=pltpu.CompilerParams(collective_id=1, has_side_effects=True, vmem_limit_bytes=limit),
        name="giveback",
    )(slots, w_part, ids)
    return grad_emb, grad_w, loss[0, 0]


def solution(mesh):
    return jax.shard_map(
        local,
        mesh=mesh,
        in_specs=(P(("dp", "bin"), None), P(("dp", "bin")), P(), P()),
        out_specs=(P(("dp", "bin"), None), P(), P()),
        check_vma=False,
    )
```

```python
import functools
import math

import jax
import jax.numpy as jnp
from jax import lax
from jax.experimental import pallas as pl
from jax.experimental.pallas import tpu as pltpu
from jax.sharding import PartitionSpec as P

MESH = pl.DeviceIdType.MESH
F32 = jnp.float32
BF16 = jnp.bfloat16
FAR = 1e30
EMPTY = 1024.0
NT = (((1,), (1,)), ((), ()))
TN = (((0,), (0,)), ((), ()))


def iota(shape, dim):
    return lax.broadcasted_iota(jnp.int32, shape, dim)


def grid_of(bins):
    chips = bins // 2
    nx = max(d for d in range(1, chips + 1) if chips % d == 0 and d * d <= chips)
    return nx, chips // nx


def hops(step, size):
    return min(step, size - step)


def plane_steps(bins):
    nx, ny = grid_of(bins)
    steps = [(dx, dy) for dx in range(nx) for dy in range(ny)]
    return sorted(steps, key=lambda d: -(hops(d[0], nx) + hops(d[1], ny)))


def turns(bins):
    ny = grid_of(bins)[1]
    codes = [2 * (dx * ny + dy) + dc for dx, dy in plane_steps(bins) for dc in range(2)]
    return [code for code in codes if code]


def back(code, bins):
    nx, ny = grid_of(bins)
    dx, dy, dc = code // (2 * ny), code // 2 % ny, code % 2
    return 2 * ((-dx % nx) * ny + -dy % ny) + dc


def chip_at(q, dx, dy, bins):
    nx, ny = grid_of(bins)
    return lax.rem(lax.div(q, ny) + dx, nx) * ny + lax.rem(lax.rem(q, ny) + dy, ny)


def device_at(me, code, bins):
    ny = grid_of(bins)[1]
    chip = chip_at(lax.div(me, 2), code // (2 * ny), code // 2 % ny, bins)
    return 2 * chip + lax.rem(lax.rem(me, 2) + code % 2, 2)


def slot_places(ids, me, bins, cap):
    nx, ny = grid_of(bins)
    half = bins // 2
    jets = ids.shape[1]
    upper = ids >= half
    chip = jnp.where(upper, ids - half, ids)
    dx = chip // ny - lax.div(me, 2 * ny)
    dx = jnp.where(dx < 0, dx + nx, dx)
    dy = chip % ny - lax.rem(lax.div(me, 2), ny)
    dy = jnp.where(dy < 0, dy + ny, dy)
    dc = jnp.where(upper, 1, 0) - lax.rem(me, 2)
    code = 2 * (dx * ny + dy) + jnp.where(dc < 0, 1, dc)
    step = 256 if jets % 256 == 0 else jets
    before = jnp.where(iota((step, step), 0) < iota((step, step), 1), 1.0, 0.0).astype(BF16)
    wide = max(bins, 16)
    carry = jnp.zeros((wide, 1), F32)
    ranks = []
    for start in range(0, jets, step):
        hot = jnp.where(code[:, start:start + step] == iota((wide, step), 0), 1.0, 0.0)
        seen = jnp.dot(hot.astype(BF16), before, preferred_element_type=F32) + carry
        ranks.append(jnp.sum(seen * hot, 0, keepdims=True))
        carry = carry + jnp.sum(hot, 1, keepdims=True)
    rank = jnp.concatenate(ranks, 1).astype(jnp.int32)
    return code * cap + rank


def line_of(ids_ref):
    return jnp.concatenate([ids_ref[r:r + 1, :] for r in range(ids_ref.shape[0])], 1)


def scatter_kernel(bins, cap, emb_hbm, ids_hbm, inbox, pinbox, counts, pcounts, outbox, emb_ref, ids_ref,
                   send, recv, fwd_send, fwd_recv, cnt_sem, loc):
    z, me = lax.axis_index("dp"), lax.axis_index("bin")
    sib = me + 1 - 2 * lax.rem(me, 2)
    jets = emb_hbm.shape[0]
    fetch_ids = pltpu.make_async_copy(ids_hbm, ids_ref, loc.at[1])
    fetch_ids.start()
    fetch = pltpu.make_async_copy(emb_hbm, emb_ref, loc.at[0])
    fetch.start()
    barrier = pltpu.get_barrier_semaphore()
    for k in range(1, bins):
        pl.semaphore_signal(barrier, inc=1, device_id=(z, lax.rem(me + k, bins)), device_id_type=MESH)
    fetch_ids.wait()
    place = slot_places(line_of(ids_ref), me, bins, cap)

    def row_copy(k):
        return pltpu.make_async_remote_copy(
            src_ref=outbox.at[k], dst_ref=inbox.at[me], send_sem=send, recv_sem=recv.at[k],
            device_id=(z, device_at(me, k, bins)), device_id_type=MESH)

    group = 8 if bins % 8 == 0 else bins
    fetch.wait()
    emb = emb_ref[...]
    solid = jnp.ones((jets, 128), BF16)
    for first in range(0, bins, group):
        rows = group * cap
        pick = jnp.where(iota((rows, jets), 0) + first * cap == place, 1.0, 0.0).astype(BF16)
        block = jnp.dot(pick, emb, preferred_element_type=F32)
        taken = jnp.dot(pick, solid, preferred_element_type=F32)
        outbox[first:first + group, :, 0:128] = jnp.where(
            taken > 0.5, block[:, 0:128], EMPTY).astype(BF16).reshape(group, cap, 128)
        outbox[first:first + group, :, 128:256] = block[:, 128:256].astype(BF16).reshape(group, cap, 128)
    pl.semaphore_wait(barrier, bins - 1)
    for k in turns(bins):
        row_copy(k).start()
    own = pltpu.make_async_copy(outbox.at[0], inbox.at[me], loc.at[1])
    own.start()

    def forward(src):
        return pltpu.make_async_remote_copy(
            src_ref=inbox.at[src], dst_ref=pinbox.at[src], send_sem=fwd_send, recv_sem=fwd_recv,
            device_id=(z, sib), device_id_type=MESH)

    def tally(src):
        live = jnp.where(inbox[src, :, 0:128].astype(F32) < EMPTY / 2, 1.0, 0.0)
        return jnp.where(iota((1, 128), 1) == src, jnp.sum(live, 0, keepdims=True), 0.0)

    own.wait()
    forward(me).start()
    table = tally(me)
    for k in turns(bins):
        row_copy(k).wait_recv()
        src = device_at(me, back(k, bins), bins)
        forward(src).start()
        table = table + tally(src)
    counts[...] = table.astype(jnp.int32)
    swap = pltpu.make_async_remote_copy(
        src_ref=counts, dst_ref=pcounts, send_sem=cnt_sem.at[0], recv_sem=cnt_sem.at[1],
        device_id=(z, sib), device_id_type=MESH)
    swap.start()
    pltpu.make_async_remote_copy(
        src_ref=outbox.at[pl.ds(1, bins - 1)], dst_ref=inbox.at[pl.ds(1, bins - 1)], send_sem=send, recv_sem=fwd_recv,
        device_id=(z, sib), device_id_type=MESH).wait_send()
    swap.wait()
    pltpu.make_async_remote_copy(
        src_ref=inbox, dst_ref=pinbox, send_sem=fwd_send, recv_sem=fwd_recv,
        device_id=(z, sib), device_id_type=MESH).wait()


def pair_kernel(bins, cap, big, cnt_ref, pcnt_ref, spread_hbm, proj_ref, mine_ref, other_ref, out_ref, w_ref,
                spread_ref, loc, xs, ys, gs, fx, fy, sax, srx, sry, inner, gram, acc, rsum, tot):
    width = proj_ref.shape[0]
    hw = width // 2
    sub = big // 2
    fetch = pltpu.make_async_copy(spread_hbm, spread_ref, loc)
    fetch.start()

    def pack(src_ref, dst, cnt):
        off = 0
        for s in range(bins):
            rows = src_ref[s].astype(F32)
            dst[0, pl.ds(off, cap), :] = rows[:, :hw]
            dst[1, pl.ds(off, cap), :] = rows[:, hw:]
            off = off + cnt[0, s]
        return off

    n_own = pack(mine_ref, xs, cnt_ref)
    n_oth = pack(other_ref, ys, pcnt_ref)
    for h in range(2):
        xs[h, pl.ds(n_own, big), :] = jnp.zeros((big, hw), F32)
    proj = proj_ref[...]
    ones = jnp.ones((8, width), BF16)
    subs_own = (n_own + sub - 1) // sub
    subs = (jnp.maximum(n_own, n_oth) + sub - 1) // sub

    def features(i, carry):
        base = pl.multiple_of(i * big, big)
        for rows_ref, feat, col_sq, row_sq, n in ((xs, fx, sax, srx, n_own), (ys, fy, None, sry, n_oth)):
            emb = jnp.concatenate([rows_ref[0, pl.ds(base, big), :], rows_ref[1, pl.ds(base, big), :]], 1)
            emb = jnp.where(iota((big, width), 0) + base < n, emb, 0.0).astype(BF16)
            val = jnp.dot(emb, proj, preferred_element_type=F32).astype(BF16)
            feat[pl.ds(base, big), :] = val
            sq = jnp.square(val.astype(F32))
            high = sq.astype(BF16)
            low = (sq - high.astype(F32)).astype(BF16)
            line = lax.dot_general(ones, high, NT, preferred_element_type=F32)
            line = line + lax.dot_general(ones, low, NT, preferred_element_type=F32)
            line = jnp.where(iota((8, big), 1) + base < n, line, FAR)
            row_sq[2 * i] = line[:, 0:sub]
            row_sq[2 * i + 1] = line[:, sub:big]
            if col_sq is not None:
                col = jnp.broadcast_to(jnp.sum(sq, 1, keepdims=True), (big, 128))
                col_sq[pl.ds(base, big), :] = jnp.where(iota((big, 128), 0) + base < n, col, FAR)
        return carry
    lax.fori_loop(0, (subs + 1) // 2, features, 0)

    fetch.wait()
    coef = [1.0 / jnp.full((8, 128), spread_ref[s], F32) / width for s in range(3)]
    rate = [c * math.log2(math.e) for c in coef]
    na = jnp.full((1, 128), jnp.maximum(n_own, 1).astype(F32), F32)
    nc = jnp.full((1, 128), jnp.maximum(n_oth, 1).astype(F32), F32)
    scale = float(bins * cap // 2 * width)
    k_self = jnp.concatenate([scale * (-(4.0 / (na * na)))] * 2, 1)
    k_cross = jnp.concatenate([scale * (4.0 / (na * nc))] * 2, 1)

    tot[...] = jnp.zeros_like(tot)
    w_ref[...] = jnp.zeros_like(w_ref)

    feats = (fx, fy)
    row_sqs = (srx, sry)

    def meet(which, rows, cols, base, col, at=0):
        xa = fx[pl.ds(base, rows), :]
        xb = feats[which][pl.ds(pl.multiple_of(col * sub, sub) + at, cols), :]
        inner[which, 0:rows, at:at + cols] = lax.dot_general(xa + xa, xb, NT, preferred_element_type=F32)

    def weigh(which, rows, cols, base, col, beside=()):
        steps = [(p, r) for p in range(0, cols, 128) for r in range(0, rows, 16)]
        beside = list(beside)
        every = max(1, len(steps) // (len(beside) + 1))
        total = jnp.zeros((8, 128), F32)
        for at, (p, r) in enumerate(steps):
            if beside and at % every == 0:
                beside.pop(0)()
            sb = row_sqs[which][col + p // sub, :, p % sub:p % sub + 128]
            parts = []
            for q in (r, r + 8):
                t = inner[which, q:q + 8, p:p + 128] - sax[pl.ds(base + q, 8), :] - sb
                e0 = jnp.exp2(t * rate[0])
                e1 = jnp.exp2(t * rate[1])
                e2 = jnp.exp2(t * rate[2])
                total = total + (e0 + e1 + e2)
                parts.append(e0 * coef[0] + e1 * coef[1] + e2 * coef[2])
            gram[which, r:r + 16, p:p + 128] = jnp.concatenate(parts, 0).astype(BF16)
        tot[which] += total
        for rest in beside:
            rest()

    def pull(which, rows, cols, col):
        xb = feats[which][pl.ds(pl.multiple_of(col * sub, sub), cols), :]
        acc[which, 0:rows, :] += jnp.dot(gram[which, 0:rows, 0:cols], xb, preferred_element_type=F32)

    def count(which, rows, cols):
        rsum[which, 0:rows, :] += jnp.dot(
            gram[which, 0:rows, 0:cols], jnp.ones((cols, 128), BF16), preferred_element_type=F32)

    def row_block(rows, base):
        acc[:, 0:rows, :] = jnp.zeros((2, rows, width), F32)
        rsum[:, 0:rows, :] = jnp.zeros((2, rows, 128), F32)
        blocks = subs // 2

        @pl.when(blocks > 0)
        def _():
            gram[1, 0:rows, :] = jnp.zeros((rows, big), BF16)
            meet(0, rows, big, base, 0)

            def turn(which, j, prev, later):
                other = 1 - which
                weigh(which, rows, big, base, 2 * j, [
                    lambda: meet(other, rows, sub, base, later, 0),
                    lambda: meet(other, rows, sub, base, later, sub),
                    lambda: pull(other, rows, big, prev),
                    lambda: count(other, rows, big)])

            def body(j, carry):
                turn(0, j, 2 * jnp.maximum(j - 1, 0), 2 * j)
                turn(1, j, 2 * j, 2 * jnp.minimum(j + 1, blocks - 1))
                return carry
            lax.fori_loop(0, blocks, body, 0)
            pull(1, rows, big, 2 * (blocks - 1))
            count(1, rows, big)

        @pl.when(subs % 2 == 1)
        def _():
            for which in (0, 1):
                meet(which, rows, sub, base, subs - 1)
            for which in (0, 1):
                weigh(which, rows, sub, base, subs - 1)
                pull(which, rows, sub, subs - 1)
                count(which, rows, sub)

        xf = fx[pl.ds(base, rows), :].astype(F32)
        force = [xf * jnp.concatenate([rsum[which, 0:rows, :]] * 2, 1) - acc[which, 0:rows, :] for which in (0, 1)]
        gz = (k_self * force[0] + k_cross * force[1]).astype(BF16)
        ge = lax.dot_general(gz, proj, NT, preferred_element_type=F32)
        gs[0, pl.ds(base, rows), :] = ge[:, :hw]
        gs[1, pl.ds(base, rows), :] = ge[:, hw:]
        emb = jnp.concatenate([xs[0, pl.ds(base, rows), :], xs[1, pl.ds(base, rows), :]], 1).astype(BF16)
        gw = lax.dot_general(emb, gz, TN, preferred_element_type=F32)
        w_ref[0, :width, :] += gw[:, :hw]
        w_ref[1, :width, :] += gw[:, hw:]

    def full(i, carry):
        row_block(big, pl.multiple_of(i * big, big))
        return carry
    lax.fori_loop(0, subs_own // 2, full, 0)

    @pl.when(subs_own % 2 == 1)
    def _():
        row_block(sub, pl.multiple_of((subs_own - 1) * sub, sub))

    for h in range(2):
        gs[h, pl.ds(n_own, cap), :] = jnp.zeros((cap, hw), F32)
    share = jnp.sum(tot[0], 0, keepdims=True) / (na * na) - jnp.sum(tot[1], 0, keepdims=True) / (na * nc)
    for h in range(2):
        w_ref[h, width:width + 8, :] = jnp.broadcast_to(share, (8, 128))
    off = 0
    for s in range(bins):
        out_ref[s, :, :hw] = gs[0, pl.ds(off, cap), :].astype(BF16)
        out_ref[s, :, hw:] = gs[1, pl.ds(off, cap), :].astype(BF16)
        off = off + cnt_ref[0, s]


def return_kernel(bins, reps, cap, slots, w_ref, ids_ref, g_out, w_out, l_out,
                  inbox, pick, p_recv, a_send, a_recv, zx, full, other,
                  send, recv, psem, asem, zsem, gsem, fsem, loc):
    z, me = lax.axis_index("dp"), lax.axis_index("bin")
    core = lax.rem(me, 2)
    q = lax.div(me, 2)
    chips = bins // 2
    sib = me + 1 - 2 * core
    jets = g_out.shape[0]
    width = g_out.shape[1]
    ar = width // chips
    tokens = float(jets * bins * reps)
    barrier = pltpu.get_barrier_semaphore()
    for k in range(1, bins):
        pl.semaphore_signal(barrier, inc=1, device_id=(z, lax.rem(me + k, bins)), device_id_type=MESH)
    for k in range(1, reps):
        pl.semaphore_signal(barrier, inc=1, device_id=(lax.rem(z + k, reps), me), device_id_type=MESH)

    place = slot_places(line_of(ids_ref), me, bins, cap)
    for first in range(0, jets, 128 if jets % 128 == 0 else jets):
        size = min(128, jets - first)
        part = jnp.broadcast_to(place[:, first:first + size], (size, size))
        column = jnp.sum(jnp.where(iota((size, size), 0) == iota((size, size), 1), part, 0), 1, keepdims=True)
        pick[first:first + size, :] = jnp.where(column == iota((size, bins * cap), 1), 1.0, 0.0).astype(BF16)
    pl.semaphore_wait(barrier, bins - 1 + reps - 1)

    def remote(src, dst, sems, dev):
        return pltpu.make_async_remote_copy(
            src_ref=src, dst_ref=dst, send_sem=sems.at[0], recv_sem=sems.at[1], device_id=dev, device_id_type=MESH)

    pair = remote(w_ref.at[1 - core], p_recv, psem, (z, sib))
    pair.start()

    def row_copy(k):
        dest = device_at(me, k, bins)
        return pltpu.make_async_remote_copy(
            src_ref=slots.at[dest], dst_ref=inbox.at[back(k, bins)], send_sem=send, recv_sem=recv,
            device_id=(z, dest), device_id_type=MESH)

    own = pltpu.make_async_copy(slots.at[me], inbox.at[0], loc)
    own.start()
    around = sorted(range(1, reps), key=lambda k: -hops(k, reps))

    pair.wait()
    loss_tile = w_ref[core, width:width + 8, :] + p_recv[width:width + 8, :]
    for k in range(chips):
        a_send[k, 0:ar, :] = w_ref[core, k * ar:(k + 1) * ar, :] + p_recv[k * ar:(k + 1) * ar, :]
        a_send[k, ar:ar + 8, :] = loss_tile

    others = [chip_at(q, dx, dy, bins) for dx, dy in plane_steps(bins) if dx or dy]
    for chip in others:
        remote(a_send.at[chip], a_recv.at[q], asem, (z, 2 * chip + core)).start()
    a_recv[q] = a_send[q]
    for k in turns(bins)[0:8]:
        row_copy(k).start()
    remote(a_send.at[pl.ds(0, chips - 1)], a_recv.at[pl.ds(0, chips - 1)], asem, (z, sib)).wait()
    for k in turns(bins)[8:24]:
        row_copy(k).start()
    chunk = a_recv[0]
    for k in range(1, chips):
        chunk = chunk + a_recv[k]
    zx[z] = chunk
    for k in around:
        remote(zx.at[z], zx.at[z], zsem, (lax.rem(z + k, reps), me)).start()
    remote(zx.at[pl.ds(0, reps - 1)], zx.at[pl.ds(0, reps - 1)], zsem, (z, sib)).wait()
    chunk = zx[0]
    for k in range(1, reps):
        chunk = chunk + zx[k]
    full[q] = chunk[0:ar, :] / tokens
    for chip in others:
        remote(full.at[q], full.at[q], gsem, (z, 2 * chip + core)).start()
    for k in turns(bins)[24:31]:
        row_copy(k).start()
    l_out[...] = jnp.broadcast_to(jnp.sum(chunk[ar:ar + 1, :], 1, keepdims=True) / reps, (1, 128))

    remote(full.at[pl.ds(0, chips - 1)], full.at[pl.ds(0, chips - 1)], gsem, (z, sib)).wait()
    last = remote(full, other, fsem, (z, sib))
    last.start()
    own.wait()
    pltpu.make_async_remote_copy(
        src_ref=slots.at[pl.ds(0, bins - 1)], dst_ref=inbox.at[pl.ds(1, bins - 1)], send_sem=send, recv_sem=recv,
        device_id=(z, sib), device_id_type=MESH).wait()
    g_out[...] = jnp.dot(pick[...], inbox[...].reshape(bins * cap, width), preferred_element_type=F32).astype(BF16)

    last.wait()
    here = full[...].reshape(width, 128)
    there = other[...].reshape(width, 128)
    w_out[:, 0:128] = jnp.where(core == 0, here, there)
    w_out[:, 128:256] = jnp.where(core == 0, there, here)


def vmem(count):
    return [pl.BlockSpec(memory_space=pltpu.VMEM)] * count


def local(embeddings, bin_ids, spreads, projection):
    jets, width = embeddings.shape
    bins, reps = lax.axis_size("bin"), lax.axis_size("dp")
    cap = 2 * jets // bins
    most = bins * cap
    chips = bins // 2
    ids = bin_ids.reshape(-1, 128) if jets % 128 == 0 else bin_ids.reshape(1, jets)
    dma = pltpu.SemaphoreType.DMA
    box = jax.ShapeDtypeStruct((bins, cap, width), BF16)
    limit = 48 << 20
    tally = jax.ShapeDtypeStruct((1, 128), jnp.int32)
    inbox, pinbox, counts, pcounts = pl.pallas_call(
        functools.partial(scatter_kernel, bins, cap),
        out_shape=(box, box, tally, tally),
        in_specs=[pl.BlockSpec(memory_space=pltpu.HBM)] * 2, out_specs=tuple(vmem(4)),
        scratch_shapes=[
            pltpu.VMEM((bins, cap, width), BF16), pltpu.VMEM((jets, width), BF16), pltpu.VMEM(ids.shape, jnp.int32),
            dma, dma((bins,)), dma, dma, dma((2,)), dma((2,))],
        compiler_params=pltpu.CompilerParams(collective_id=0, has_side_effects=True, vmem_limit_bytes=limit),
        name="scatter",
    )(embeddings, ids)

    big = 512
    top = -(-most // big) * big
    room = top + big
    slots, w_part = pl.pallas_call(
        functools.partial(pair_kernel, bins, cap, big),
        out_shape=(box, jax.ShapeDtypeStruct((2, width + 8, 128), F32)),
        in_specs=[pl.BlockSpec(memory_space=pltpu.SMEM)] * 2 + [pl.BlockSpec(memory_space=pltpu.HBM)] + vmem(3),
        out_specs=tuple(vmem(2)),
        scratch_shapes=[
            pltpu.SMEM((3,), F32), dma,
            pltpu.VMEM((2, room, width // 2), F32), pltpu.VMEM((2, room, width // 2), F32),
            pltpu.VMEM((2, room, width // 2), F32),
            pltpu.VMEM((top, width), BF16), pltpu.VMEM((top, width), BF16), pltpu.VMEM((top, 128), F32),
            pltpu.VMEM((2 * top // big, 8, big // 2), F32), pltpu.VMEM((2 * top // big, 8, big // 2), F32),
            pltpu.VMEM((2, big, big), F32), pltpu.VMEM((2, big, big), BF16),
            pltpu.VMEM((2, big, width), F32), pltpu.VMEM((2, big, 128), F32), pltpu.VMEM((2, 8, 128), F32)],
        compiler_params=pltpu.CompilerParams(vmem_limit_bytes=limit),
        name="pairs",
    )(counts, pcounts, spreads, projection, inbox, pinbox)

    ar = width // chips
    grad_emb, grad_w, loss = pl.pallas_call(
        functools.partial(return_kernel, bins, reps, cap),
        out_shape=(jax.ShapeDtypeStruct((jets, width), BF16), jax.ShapeDtypeStruct((width, width), F32),
                   jax.ShapeDtypeStruct((1, 128), F32)),
        in_specs=vmem(3), out_specs=tuple(vmem(3)),
        scratch_shapes=[
            pltpu.VMEM((bins, cap, width), BF16), pltpu.VMEM((jets, most), BF16),
            pltpu.VMEM((width + 8, 128), F32),
            pltpu.VMEM((chips, ar + 8, 128), F32), pltpu.VMEM((chips, ar + 8, 128), F32),
            pltpu.VMEM((reps, ar + 8, 128), F32), pltpu.VMEM((chips, ar, 128), F32), pltpu.VMEM((chips, ar, 128), F32),
            dma, dma, dma((2,)), dma((2,)), dma((2,)), dma((2,)), dma((2,)), dma],
        compiler_params=pltpu.CompilerParams(collective_id=1, has_side_effects=True, vmem_limit_bytes=limit),
        name="giveback",
    )(slots, w_part, ids)
    return grad_emb, grad_w, loss[0, 0]


def solution(mesh):
    return jax.shard_map(
        local,
        mesh=mesh,
        in_specs=(P(("dp", "bin"), None), P(("dp", "bin")), P(), P()),
        out_specs=(P(("dp", "bin"), None), P(), P()),
        check_vma=False,
    )
```

```python
import functools
import math

import jax
import jax.numpy as jnp
from jax import lax
from jax.experimental import pallas as pl
from jax.experimental.pallas import tpu as pltpu
from jax.sharding import PartitionSpec as P

MESH = pl.DeviceIdType.MESH
F32 = jnp.float32
BF16 = jnp.bfloat16
FAR = 1e30
EMPTY = 1024.0
NT = (((1,), (1,)), ((), ()))
TN = (((0,), (0,)), ((), ()))


def iota(shape, dim):
    return lax.broadcasted_iota(jnp.int32, shape, dim)


def grid_of(bins):
    chips = bins // 2
    nx = max(d for d in range(1, chips + 1) if chips % d == 0 and d * d <= chips)
    return nx, chips // nx


def hops(step, size):
    return min(step, size - step)


def plane_steps(bins):
    nx, ny = grid_of(bins)
    steps = [(dx, dy) for dx in range(nx) for dy in range(ny)]
    return sorted(steps, key=lambda d: -(hops(d[0], nx) + hops(d[1], ny)))


def turns(bins):
    ny = grid_of(bins)[1]
    codes = [2 * (dx * ny + dy) + dc for dx, dy in plane_steps(bins) for dc in range(2)]
    return [code for code in codes if code]


def back(code, bins):
    nx, ny = grid_of(bins)
    dx, dy, dc = code // (2 * ny), code // 2 % ny, code % 2
    return 2 * ((-dx % nx) * ny + -dy % ny) + dc


def chip_at(q, dx, dy, bins):
    nx, ny = grid_of(bins)
    return lax.rem(lax.div(q, ny) + dx, nx) * ny + lax.rem(lax.rem(q, ny) + dy, ny)


def device_at(me, code, bins):
    ny = grid_of(bins)[1]
    chip = chip_at(lax.div(me, 2), code // (2 * ny), code // 2 % ny, bins)
    return 2 * chip + lax.rem(lax.rem(me, 2) + code % 2, 2)


def slot_places(ids, me, bins, cap):
    nx, ny = grid_of(bins)
    half = bins // 2
    jets = ids.shape[1]
    upper = ids >= half
    chip = jnp.where(upper, ids - half, ids)
    dx = chip // ny - lax.div(me, 2 * ny)
    dx = jnp.where(dx < 0, dx + nx, dx)
    dy = chip % ny - lax.rem(lax.div(me, 2), ny)
    dy = jnp.where(dy < 0, dy + ny, dy)
    dc = jnp.where(upper, 1, 0) - lax.rem(me, 2)
    code = 2 * (dx * ny + dy) + jnp.where(dc < 0, 1, dc)
    step = 256 if jets % 256 == 0 else jets
    before = jnp.where(iota((step, step), 0) < iota((step, step), 1), 1.0, 0.0).astype(BF16)
    wide = max(bins, 16)
    carry = jnp.zeros((wide, 1), F32)
    ranks = []
    for start in range(0, jets, step):
        hot = jnp.where(code[:, start:start + step] == iota((wide, step), 0), 1.0, 0.0)
        seen = jnp.dot(hot.astype(BF16), before, preferred_element_type=F32) + carry
        ranks.append(jnp.sum(seen * hot, 0, keepdims=True))
        carry = carry + jnp.sum(hot, 1, keepdims=True)
    rank = jnp.concatenate(ranks, 1).astype(jnp.int32)
    return code * cap + rank


def line_of(ids_ref):
    return jnp.concatenate([ids_ref[r:r + 1, :] for r in range(ids_ref.shape[0])], 1)


def scatter_kernel(bins, cap, emb_hbm, ids_hbm, inbox, pinbox, counts, pcounts, outbox, emb_ref, ids_ref,
                   send, recv, fwd_send, fwd_recv, cnt_sem, loc):
    z, me = lax.axis_index("dp"), lax.axis_index("bin")
    sib = me + 1 - 2 * lax.rem(me, 2)
    jets = emb_hbm.shape[0]
    fetch_ids = pltpu.make_async_copy(ids_hbm, ids_ref, loc.at[1])
    fetch_ids.start()
    fetch = pltpu.make_async_copy(emb_hbm, emb_ref, loc.at[0])
    fetch.start()
    barrier = pltpu.get_barrier_semaphore()
    for k in range(1, bins):
        pl.semaphore_signal(barrier, inc=1, device_id=(z, lax.rem(me + k, bins)), device_id_type=MESH)
    fetch_ids.wait()
    place = slot_places(line_of(ids_ref), me, bins, cap)

    def row_copy(k):
        return pltpu.make_async_remote_copy(
            src_ref=outbox.at[k], dst_ref=inbox.at[me], send_sem=send, recv_sem=recv.at[k],
            device_id=(z, device_at(me, k, bins)), device_id_type=MESH)

    group = 8 if bins % 8 == 0 else bins
    fetch.wait()
    emb = emb_ref[...]
    solid = jnp.ones((jets, 128), BF16)
    for first in range(0, bins, group):
        rows = group * cap
        pick = jnp.where(iota((rows, jets), 0) + first * cap == place, 1.0, 0.0).astype(BF16)
        block = jnp.dot(pick, emb, preferred_element_type=F32)
        taken = jnp.dot(pick, solid, preferred_element_type=F32)
        outbox[first:first + group, :, 0:128] = jnp.where(
            taken > 0.5, block[:, 0:128], EMPTY).astype(BF16).reshape(group, cap, 128)
        outbox[first:first + group, :, 128:256] = block[:, 128:256].astype(BF16).reshape(group, cap, 128)
    pl.semaphore_wait(barrier, bins - 1)
    for k in turns(bins):
        row_copy(k).start()
    own = pltpu.make_async_copy(outbox.at[0], inbox.at[me], loc.at[1])
    own.start()

    def forward(src):
        return pltpu.make_async_remote_copy(
            src_ref=inbox.at[src], dst_ref=pinbox.at[src], send_sem=fwd_send, recv_sem=fwd_recv,
            device_id=(z, sib), device_id_type=MESH)

    def tally(src):
        live = jnp.where(inbox[src, :, 0:128].astype(F32) < EMPTY / 2, 1.0, 0.0)
        return jnp.where(iota((1, 128), 1) == src, jnp.sum(live, 0, keepdims=True), 0.0)

    own.wait()
    forward(me).start()
    table = tally(me)
    for k in turns(bins):
        row_copy(k).wait_recv()
        src = device_at(me, back(k, bins), bins)
        forward(src).start()
        table = table + tally(src)
    counts[...] = table.astype(jnp.int32)
    swap = pltpu.make_async_remote_copy(
        src_ref=counts, dst_ref=pcounts, send_sem=cnt_sem.at[0], recv_sem=cnt_sem.at[1],
        device_id=(z, sib), device_id_type=MESH)
    swap.start()
    pltpu.make_async_remote_copy(
        src_ref=outbox.at[pl.ds(1, bins - 1)], dst_ref=inbox.at[pl.ds(1, bins - 1)], send_sem=send, recv_sem=fwd_recv,
        device_id=(z, sib), device_id_type=MESH).wait_send()
    swap.wait()
    pltpu.make_async_remote_copy(
        src_ref=inbox, dst_ref=pinbox, send_sem=fwd_send, recv_sem=fwd_recv,
        device_id=(z, sib), device_id_type=MESH).wait()


def pair_kernel(bins, cap, big, cnt_ref, pcnt_ref, spread_hbm, proj_ref, mine_ref, other_ref, out_ref, w_ref,
                spread_ref, loc, xs, ys, gs, fx, fy, sax, srx, sry, inner, gram, acc, rsum, tot):
    width = proj_ref.shape[0]
    hw = width // 2
    sub = big // 2
    fetch = pltpu.make_async_copy(spread_hbm, spread_ref, loc)
    fetch.start()

    def pack(src_ref, dst, cnt):
        off = 0
        for s in range(bins):
            rows = src_ref[s].astype(F32)
            dst[0, pl.ds(off, cap), :] = rows[:, :hw]
            dst[1, pl.ds(off, cap), :] = rows[:, hw:]
            off = off + cnt[0, s]
        return off

    n_own = pack(mine_ref, xs, cnt_ref)
    n_oth = pack(other_ref, ys, pcnt_ref)
    for h in range(2):
        xs[h, pl.ds(n_own, big), :] = jnp.zeros((big, hw), F32)
    proj = proj_ref[...]
    ones = jnp.ones((8, width), BF16)
    subs_own = (n_own + sub - 1) // sub
    subs = (jnp.maximum(n_own, n_oth) + sub - 1) // sub

    def features(i, carry):
        base = pl.multiple_of(i * big, big)
        for rows_ref, feat, col_sq, row_sq, n in ((xs, fx, sax, srx, n_own), (ys, fy, None, sry, n_oth)):
            emb = jnp.concatenate([rows_ref[0, pl.ds(base, big), :], rows_ref[1, pl.ds(base, big), :]], 1)
            emb = jnp.where(iota((big, width), 0) + base < n, emb, 0.0).astype(BF16)
            val = jnp.dot(emb, proj, preferred_element_type=F32).astype(BF16)
            feat[pl.ds(base, big), :] = val
            sq = jnp.square(val.astype(F32))
            high = sq.astype(BF16)
            low = (sq - high.astype(F32)).astype(BF16)
            line = lax.dot_general(ones, high, NT, preferred_element_type=F32)
            line = line + lax.dot_general(ones, low, NT, preferred_element_type=F32)
            line = jnp.where(iota((8, big), 1) + base < n, line, FAR)
            row_sq[2 * i] = line[:, 0:sub]
            row_sq[2 * i + 1] = line[:, sub:big]
            if col_sq is not None:
                col = jnp.broadcast_to(jnp.sum(sq, 1, keepdims=True), (big, 128))
                col_sq[pl.ds(base, big), :] = jnp.where(iota((big, 128), 0) + base < n, col, FAR)
        return carry
    lax.fori_loop(0, (subs + 1) // 2, features, 0)

    fetch.wait()
    coef = [1.0 / jnp.full((8, 128), spread_ref[s], F32) / width for s in range(3)]
    rate = [c * math.log2(math.e) for c in coef]
    na = jnp.full((1, 128), jnp.maximum(n_own, 1).astype(F32), F32)
    nc = jnp.full((1, 128), jnp.maximum(n_oth, 1).astype(F32), F32)
    scale = float(bins * cap // 2 * width)
    k_self = jnp.concatenate([scale * (-(4.0 / (na * na)))] * 2, 1)
    k_cross = jnp.concatenate([scale * (4.0 / (na * nc))] * 2, 1)

    tot[...] = jnp.zeros_like(tot)
    w_ref[...] = jnp.zeros_like(w_ref)

    feats = (fx, fy)
    row_sqs = (srx, sry)

    def meet(which, rows, cols, base, col, at=0):
        xa = fx[pl.ds(base, rows), :]
        xb = feats[which][pl.ds(pl.multiple_of(col * sub, sub) + at, cols), :]
        inner[which, 0:rows, at:at + cols] = lax.dot_general(xa + xa, xb, NT, preferred_element_type=F32)

    def weigh(which, rows, cols, base, col, beside=()):
        steps = [(p, r) for p in range(0, cols, 128) for r in range(0, rows, 16)]
        beside = list(beside)
        every = max(1, len(steps) // (len(beside) + 1))
        total = jnp.zeros((8, 128), F32)
        for at, (p, r) in enumerate(steps):
            if beside and at % every == 0:
                beside.pop(0)()
            sb = row_sqs[which][col + p // sub, :, p % sub:p % sub + 128]
            parts = []
            for q in (r, r + 8):
                t = inner[which, q:q + 8, p:p + 128] - sax[pl.ds(base + q, 8), :] - sb
                e0 = jnp.exp2(t * rate[0])
                e1 = jnp.exp2(t * rate[1])
                e2 = jnp.exp2(t * rate[2])
                total = total + (e0 + e1 + e2)
                parts.append(e0 * coef[0] + e1 * coef[1] + e2 * coef[2])
            gram[which, r:r + 16, p:p + 128] = jnp.concatenate(parts, 0).astype(BF16)
        tot[which] += total
        for rest in beside:
            rest()

    def pull(which, rows, cols, col):
        xb = feats[which][pl.ds(pl.multiple_of(col * sub, sub), cols), :]
        acc[which, 0:rows, :] += jnp.dot(gram[which, 0:rows, 0:cols], xb, preferred_element_type=F32)

    def count(which, rows, cols):
        rsum[which, 0:rows, :] += jnp.dot(
            gram[which, 0:rows, 0:cols], jnp.ones((cols, 128), BF16), preferred_element_type=F32)

    def row_block(rows, base):
        acc[:, 0:rows, :] = jnp.zeros((2, rows, width), F32)
        rsum[:, 0:rows, :] = jnp.zeros((2, rows, 128), F32)
        blocks = subs // 2

        @pl.when(blocks > 0)
        def _():
            gram[1, 0:rows, :] = jnp.zeros((rows, big), BF16)
            meet(0, rows, big, base, 0)

            def turn(which, j, prev, later):
                other = 1 - which
                weigh(which, rows, big, base, 2 * j, [
                    lambda: meet(other, rows, sub, base, later, 0),
                    lambda: meet(other, rows, sub, base, later, sub),
                    lambda: pull(other, rows, big, prev),
                    lambda: count(other, rows, big)])

            def body(j, carry):
                turn(0, j, 2 * jnp.maximum(j - 1, 0), 2 * j)
                turn(1, j, 2 * j, 2 * jnp.minimum(j + 1, blocks - 1))
                return carry
            lax.fori_loop(0, blocks, body, 0)
            pull(1, rows, big, 2 * (blocks - 1))
            count(1, rows, big)

        @pl.when(subs % 2 == 1)
        def _():
            for which in (0, 1):
                meet(which, rows, sub, base, subs - 1)
            for which in (0, 1):
                weigh(which, rows, sub, base, subs - 1)
                pull(which, rows, sub, subs - 1)
                count(which, rows, sub)

        xf = fx[pl.ds(base, rows), :].astype(F32)
        force = [xf * jnp.concatenate([rsum[which, 0:rows, :]] * 2, 1) - acc[which, 0:rows, :] for which in (0, 1)]
        gz = (k_self * force[0] + k_cross * force[1]).astype(BF16)
        ge = lax.dot_general(gz, proj, NT, preferred_element_type=F32)
        gs[0, pl.ds(base, rows), :] = ge[:, :hw]
        gs[1, pl.ds(base, rows), :] = ge[:, hw:]
        emb = jnp.concatenate([xs[0, pl.ds(base, rows), :], xs[1, pl.ds(base, rows), :]], 1).astype(BF16)
        gw = lax.dot_general(emb, gz, TN, preferred_element_type=F32)
        w_ref[0, :width, :] += gw[:, :hw]
        w_ref[1, :width, :] += gw[:, hw:]

    def full(i, carry):
        row_block(big, pl.multiple_of(i * big, big))
        return carry
    lax.fori_loop(0, subs_own // 2, full, 0)

    @pl.when(subs_own % 2 == 1)
    def _():
        row_block(sub, pl.multiple_of((subs_own - 1) * sub, sub))

    for h in range(2):
        gs[h, pl.ds(n_own, cap), :] = jnp.zeros((cap, hw), F32)
    share = jnp.sum(tot[0], 0, keepdims=True) / (na * na) - jnp.sum(tot[1], 0, keepdims=True) / (na * nc)
    for h in range(2):
        w_ref[h, width:width + 8, :] = jnp.broadcast_to(share, (8, 128))
    off = 0
    for s in range(bins):
        out_ref[s, :, :hw] = gs[0, pl.ds(off, cap), :].astype(BF16)
        out_ref[s, :, hw:] = gs[1, pl.ds(off, cap), :].astype(BF16)
        off = off + cnt_ref[0, s]


def return_kernel(bins, reps, cap, slots, w_ref, ids_ref, g_out, w_out, l_out,
                  inbox, pick, p_recv, a_send, a_recv, zx, full, other,
                  send, recv, psem, asem, zsem, gsem, fsem, loc):
    z, me = lax.axis_index("dp"), lax.axis_index("bin")
    core = lax.rem(me, 2)
    q = lax.div(me, 2)
    chips = bins // 2
    sib = me + 1 - 2 * core
    jets = g_out.shape[0]
    width = g_out.shape[1]
    ar = width // chips
    tokens = float(jets * bins * reps)
    barrier = pltpu.get_barrier_semaphore()
    for k in range(1, bins):
        pl.semaphore_signal(barrier, inc=1, device_id=(z, lax.rem(me + k, bins)), device_id_type=MESH)
    for k in range(1, reps):
        pl.semaphore_signal(barrier, inc=1, device_id=(lax.rem(z + k, reps), me), device_id_type=MESH)

    place = slot_places(line_of(ids_ref), me, bins, cap)
    for first in range(0, jets, 128 if jets % 128 == 0 else jets):
        size = min(128, jets - first)
        part = jnp.broadcast_to(place[:, first:first + size], (size, size))
        column = jnp.sum(jnp.where(iota((size, size), 0) == iota((size, size), 1), part, 0), 1, keepdims=True)
        pick[first:first + size, :] = jnp.where(column == iota((size, bins * cap), 1), 1.0, 0.0).astype(BF16)
    pl.semaphore_wait(barrier, bins - 1 + reps - 1)

    def remote(src, dst, sems, dev):
        return pltpu.make_async_remote_copy(
            src_ref=src, dst_ref=dst, send_sem=sems.at[0], recv_sem=sems.at[1], device_id=dev, device_id_type=MESH)

    pair = remote(w_ref.at[1 - core], p_recv, psem, (z, sib))
    pair.start()

    def row_copy(k):
        dest = device_at(me, k, bins)
        return pltpu.make_async_remote_copy(
            src_ref=slots.at[dest], dst_ref=inbox.at[back(k, bins)], send_sem=send, recv_sem=recv,
            device_id=(z, dest), device_id_type=MESH)

    own = pltpu.make_async_copy(slots.at[me], inbox.at[0], loc)
    own.start()
    around = sorted(range(1, reps), key=lambda k: -hops(k, reps))

    pair.wait()
    loss_tile = w_ref[core, width:width + 1, :] + p_recv[width:width + 1, :]
    for k in range(chips):
        a_send[k, 0:ar, :] = w_ref[core, k * ar:(k + 1) * ar, :] + p_recv[k * ar:(k + 1) * ar, :]
        a_send[k, ar:ar + 1, :] = loss_tile

    others = [chip_at(q, dx, dy, bins) for dx, dy in plane_steps(bins) if dx or dy]
    for chip in others:
        remote(a_send.at[chip], a_recv.at[q], asem, (z, 2 * chip + core)).start()
    a_recv[q] = a_send[q]
    for k in turns(bins)[0:8]:
        row_copy(k).start()
    remote(a_send.at[pl.ds(0, chips - 1)], a_recv.at[pl.ds(0, chips - 1)], asem, (z, sib)).wait()
    for k in turns(bins)[8:24]:
        row_copy(k).start()
    chunk = a_recv[0]
    for k in range(1, chips):
        chunk = chunk + a_recv[k]
    zx[z] = chunk
    for k in around:
        remote(zx.at[z], zx.at[z], zsem, (lax.rem(z + k, reps), me)).start()
    remote(zx.at[pl.ds(0, reps - 1)], zx.at[pl.ds(0, reps - 1)], zsem, (z, sib)).wait()
    chunk = zx[0]
    for k in range(1, reps):
        chunk = chunk + zx[k]
    full[q] = chunk[0:ar, :] / tokens
    for chip in others:
        remote(full.at[q], full.at[q], gsem, (z, 2 * chip + core)).start()
    for k in turns(bins)[24:31]:
        row_copy(k).start()
    l_out[...] = jnp.broadcast_to(jnp.sum(chunk[ar:ar + 1, :], 1, keepdims=True) / reps, (1, 128))

    remote(full.at[pl.ds(0, chips - 1)], full.at[pl.ds(0, chips - 1)], gsem, (z, sib)).wait()
    last = remote(full, other, fsem, (z, sib))
    last.start()
    own.wait()
    pltpu.make_async_remote_copy(
        src_ref=slots.at[pl.ds(0, bins - 1)], dst_ref=inbox.at[pl.ds(1, bins - 1)], send_sem=send, recv_sem=recv,
        device_id=(z, sib), device_id_type=MESH).wait()
    g_out[...] = jnp.dot(pick[...], inbox[...].reshape(bins * cap, width), preferred_element_type=F32).astype(BF16)

    last.wait()
    here = full[...].reshape(width, 128)
    there = other[...].reshape(width, 128)
    w_out[:, 0:128] = jnp.where(core == 0, here, there)
    w_out[:, 128:256] = jnp.where(core == 0, there, here)


def vmem(count):
    return [pl.BlockSpec(memory_space=pltpu.VMEM)] * count


def local(embeddings, bin_ids, spreads, projection):
    jets, width = embeddings.shape
    bins, reps = lax.axis_size("bin"), lax.axis_size("dp")
    cap = 2 * jets // bins
    most = bins * cap
    chips = bins // 2
    ids = bin_ids.reshape(-1, 128) if jets % 128 == 0 else bin_ids.reshape(1, jets)
    dma = pltpu.SemaphoreType.DMA
    box = jax.ShapeDtypeStruct((bins, cap, width), BF16)
    limit = 48 << 20
    tally = jax.ShapeDtypeStruct((1, 128), jnp.int32)
    inbox, pinbox, counts, pcounts = pl.pallas_call(
        functools.partial(scatter_kernel, bins, cap),
        out_shape=(box, box, tally, tally),
        in_specs=[pl.BlockSpec(memory_space=pltpu.HBM)] * 2, out_specs=tuple(vmem(4)),
        scratch_shapes=[
            pltpu.VMEM((bins, cap, width), BF16), pltpu.VMEM((jets, width), BF16), pltpu.VMEM(ids.shape, jnp.int32),
            dma, dma((bins,)), dma, dma, dma((2,)), dma((2,))],
        compiler_params=pltpu.CompilerParams(collective_id=0, has_side_effects=True, vmem_limit_bytes=limit),
        name="scatter",
    )(embeddings, ids)

    big = 512
    top = -(-most // big) * big
    room = top + big
    slots, w_part = pl.pallas_call(
        functools.partial(pair_kernel, bins, cap, big),
        out_shape=(box, jax.ShapeDtypeStruct((2, width + 8, 128), F32)),
        in_specs=[pl.BlockSpec(memory_space=pltpu.SMEM)] * 2 + [pl.BlockSpec(memory_space=pltpu.HBM)] + vmem(3),
        out_specs=tuple(vmem(2)),
        scratch_shapes=[
            pltpu.SMEM((3,), F32), dma,
            pltpu.VMEM((2, room, width // 2), F32), pltpu.VMEM((2, room, width // 2), F32),
            pltpu.VMEM((2, room, width // 2), F32),
            pltpu.VMEM((top, width), BF16), pltpu.VMEM((top, width), BF16), pltpu.VMEM((top, 128), F32),
            pltpu.VMEM((2 * top // big, 8, big // 2), F32), pltpu.VMEM((2 * top // big, 8, big // 2), F32),
            pltpu.VMEM((2, big, big), F32), pltpu.VMEM((2, big, big), BF16),
            pltpu.VMEM((2, big, width), F32), pltpu.VMEM((2, big, 128), F32), pltpu.VMEM((2, 8, 128), F32)],
        compiler_params=pltpu.CompilerParams(vmem_limit_bytes=limit),
        name="pairs",
    )(counts, pcounts, spreads, projection, inbox, pinbox)

    ar = width // chips
    grad_emb, grad_w, loss = pl.pallas_call(
        functools.partial(return_kernel, bins, reps, cap),
        out_shape=(jax.ShapeDtypeStruct((jets, width), BF16), jax.ShapeDtypeStruct((width, width), F32),
                   jax.ShapeDtypeStruct((1, 128), F32)),
        in_specs=vmem(3), out_specs=tuple(vmem(3)),
        scratch_shapes=[
            pltpu.VMEM((bins, cap, width), BF16), pltpu.VMEM((jets, most), BF16),
            pltpu.VMEM((width + 8, 128), F32),
            pltpu.VMEM((chips, ar + 1, 128), F32), pltpu.VMEM((chips, ar + 1, 128), F32),
            pltpu.VMEM((reps, ar + 1, 128), F32), pltpu.VMEM((chips, ar, 128), F32), pltpu.VMEM((chips, ar, 128), F32),
            dma, dma, dma((2,)), dma((2,)), dma((2,)), dma((2,)), dma((2,)), dma],
        compiler_params=pltpu.CompilerParams(collective_id=1, has_side_effects=True, vmem_limit_bytes=limit),
        name="giveback",
    )(slots, w_part, ids)
    return grad_emb, grad_w, loss[0, 0]


def solution(mesh):
    return jax.shard_map(
        local,
        mesh=mesh,
        in_specs=(P(("dp", "bin"), None), P(("dp", "bin")), P(), P()),
        out_specs=(P(("dp", "bin"), None), P(), P()),
        check_vma=False,
    )
```

```python
import functools
import math

import jax
import jax.numpy as jnp
from jax import lax
from jax.experimental import pallas as pl
from jax.experimental.pallas import tpu as pltpu
from jax.sharding import PartitionSpec as P

MESH = pl.DeviceIdType.MESH
F32 = jnp.float32
BF16 = jnp.bfloat16
FAR = 1e30
EMPTY = 1024.0
NT = (((1,), (1,)), ((), ()))
TN = (((0,), (0,)), ((), ()))


def iota(shape, dim):
    return lax.broadcasted_iota(jnp.int32, shape, dim)


def grid_of(bins):
    chips = bins // 2
    nx = max(d for d in range(1, chips + 1) if chips % d == 0 and d * d <= chips)
    return nx, chips // nx


def hops(step, size):
    return min(step, size - step)


def plane_steps(bins):
    nx, ny = grid_of(bins)
    steps = [(dx, dy) for dx in range(nx) for dy in range(ny)]
    return sorted(steps, key=lambda d: -(hops(d[0], nx) + hops(d[1], ny)))


def turns(bins):
    ny = grid_of(bins)[1]
    codes = [2 * (dx * ny + dy) + dc for dx, dy in plane_steps(bins) for dc in range(2)]
    return [code for code in codes if code]


def back(code, bins):
    nx, ny = grid_of(bins)
    dx, dy, dc = code // (2 * ny), code // 2 % ny, code % 2
    return 2 * ((-dx % nx) * ny + -dy % ny) + dc


def chip_at(q, dx, dy, bins):
    nx, ny = grid_of(bins)
    return lax.rem(lax.div(q, ny) + dx, nx) * ny + lax.rem(lax.rem(q, ny) + dy, ny)


def device_at(me, code, bins):
    ny = grid_of(bins)[1]
    chip = chip_at(lax.div(me, 2), code // (2 * ny), code // 2 % ny, bins)
    return 2 * chip + lax.rem(lax.rem(me, 2) + code % 2, 2)


def slot_places(ids, me, bins, cap):
    nx, ny = grid_of(bins)
    half = bins // 2
    jets = ids.shape[1]
    upper = ids >= half
    chip = jnp.where(upper, ids - half, ids)
    dx = chip // ny - lax.div(me, 2 * ny)
    dx = jnp.where(dx < 0, dx + nx, dx)
    dy = chip % ny - lax.rem(lax.div(me, 2), ny)
    dy = jnp.where(dy < 0, dy + ny, dy)
    dc = jnp.where(upper, 1, 0) - lax.rem(me, 2)
    code = 2 * (dx * ny + dy) + jnp.where(dc < 0, 1, dc)
    step = 256 if jets % 256 == 0 else jets
    before = jnp.where(iota((step, step), 0) < iota((step, step), 1), 1.0, 0.0).astype(BF16)
    wide = max(bins, 16)
    carry = jnp.zeros((wide, 1), F32)
    ranks = []
    for start in range(0, jets, step):
        hot = jnp.where(code[:, start:start + step] == iota((wide, step), 0), 1.0, 0.0)
        seen = jnp.dot(hot.astype(BF16), before, preferred_element_type=F32) + carry
        ranks.append(jnp.sum(seen * hot, 0, keepdims=True))
        carry = carry + jnp.sum(hot, 1, keepdims=True)
    rank = jnp.concatenate(ranks, 1).astype(jnp.int32)
    return code * cap + rank


def line_of(ids_ref):
    return jnp.concatenate([ids_ref[r:r + 1, :] for r in range(ids_ref.shape[0])], 1)


def scatter_kernel(bins, cap, emb_ref, ids_ref, inbox, pinbox, counts, pcounts, outbox,
                   send, recv, fwd_send, fwd_recv, cnt_sem, loc):
    z, me = lax.axis_index("dp"), lax.axis_index("bin")
    sib = me + 1 - 2 * lax.rem(me, 2)
    jets = emb_ref.shape[0]
    barrier = pltpu.get_barrier_semaphore()
    for k in range(1, bins):
        pl.semaphore_signal(barrier, inc=1, device_id=(z, lax.rem(me + k, bins)), device_id_type=MESH)
    place = slot_places(line_of(ids_ref), me, bins, cap)

    def row_copy(k):
        return pltpu.make_async_remote_copy(
            src_ref=outbox.at[k], dst_ref=inbox.at[me], send_sem=send, recv_sem=recv.at[k],
            device_id=(z, device_at(me, k, bins)), device_id_type=MESH)

    group = 8 if bins % 8 == 0 else bins
    emb = emb_ref[...]
    solid = jnp.ones((jets, 128), BF16)
    for first in range(0, bins, group):
        rows = group * cap
        pick = jnp.where(iota((rows, jets), 0) + first * cap == place, 1.0, 0.0).astype(BF16)
        block = jnp.dot(pick, emb, preferred_element_type=F32)
        taken = jnp.dot(pick, solid, preferred_element_type=F32)
        outbox[first:first + group, :, 0:128] = jnp.where(
            taken > 0.5, block[:, 0:128], EMPTY).astype(BF16).reshape(group, cap, 128)
        outbox[first:first + group, :, 128:256] = block[:, 128:256].astype(BF16).reshape(group, cap, 128)
    pl.semaphore_wait(barrier, bins - 1)
    for k in turns(bins):
        row_copy(k).start()
    own = pltpu.make_async_copy(outbox.at[0], inbox.at[me], loc)
    own.start()

    def forward(src):
        return pltpu.make_async_remote_copy(
            src_ref=inbox.at[src], dst_ref=pinbox.at[src], send_sem=fwd_send, recv_sem=fwd_recv,
            device_id=(z, sib), device_id_type=MESH)

    def tally(src):
        live = jnp.where(inbox[src, :, 0:128].astype(F32) < EMPTY / 2, 1.0, 0.0)
        return jnp.where(iota((1, 128), 1) == src, jnp.sum(live, 0, keepdims=True), 0.0)

    own.wait()
    forward(me).start()
    table = tally(me)
    for k in turns(bins):
        row_copy(k).wait_recv()
        src = device_at(me, back(k, bins), bins)
        forward(src).start()
        table = table + tally(src)
    counts[...] = table.astype(jnp.int32)
    swap = pltpu.make_async_remote_copy(
        src_ref=counts, dst_ref=pcounts, send_sem=cnt_sem.at[0], recv_sem=cnt_sem.at[1],
        device_id=(z, sib), device_id_type=MESH)
    swap.start()
    pltpu.make_async_remote_copy(
        src_ref=outbox.at[pl.ds(1, bins - 1)], dst_ref=inbox.at[pl.ds(1, bins - 1)], send_sem=send, recv_sem=fwd_recv,
        device_id=(z, sib), device_id_type=MESH).wait_send()
    swap.wait()
    pltpu.make_async_remote_copy(
        src_ref=inbox, dst_ref=pinbox, send_sem=fwd_send, recv_sem=fwd_recv,
        device_id=(z, sib), device_id_type=MESH).wait()


def pair_kernel(bins, cap, big, cnt_ref, pcnt_ref, spread_hbm, proj_ref, mine_ref, other_ref, out_ref, w_ref,
                spread_ref, loc, xs, ys, gs, fx, fy, sax, srx, sry, inner, gram, acc, rsum, tot):
    width = proj_ref.shape[0]
    hw = width // 2
    sub = big // 2
    fetch = pltpu.make_async_copy(spread_hbm, spread_ref, loc)
    fetch.start()

    def pack(src_ref, dst, cnt):
        off = 0
        for s in range(bins):
            rows = src_ref[s].astype(F32)
            dst[0, pl.ds(off, cap), :] = rows[:, :hw]
            dst[1, pl.ds(off, cap), :] = rows[:, hw:]
            off = off + cnt[0, s]
        return off

    n_own = pack(mine_ref, xs, cnt_ref)
    n_oth = pack(other_ref, ys, pcnt_ref)
    for h in range(2):
        xs[h, pl.ds(n_own, big), :] = jnp.zeros((big, hw), F32)
    proj = proj_ref[...]
    ones = jnp.ones((8, width), BF16)
    subs_own = (n_own + sub - 1) // sub
    subs = (jnp.maximum(n_own, n_oth) + sub - 1) // sub

    def features(i, carry):
        base = pl.multiple_of(i * big, big)
        for rows_ref, feat, col_sq, row_sq, n in ((xs, fx, sax, srx, n_own), (ys, fy, None, sry, n_oth)):
            emb = jnp.concatenate([rows_ref[0, pl.ds(base, big), :], rows_ref[1, pl.ds(base, big), :]], 1)
            emb = jnp.where(iota((big, width), 0) + base < n, emb, 0.0).astype(BF16)
            val = jnp.dot(emb, proj, preferred_element_type=F32).astype(BF16)
            feat[pl.ds(base, big), :] = val
            sq = jnp.square(val.astype(F32))
            high = sq.astype(BF16)
            low = (sq - high.astype(F32)).astype(BF16)
            line = lax.dot_general(ones, high, NT, preferred_element_type=F32)
            line = line + lax.dot_general(ones, low, NT, preferred_element_type=F32)
            line = jnp.where(iota((8, big), 1) + base < n, line, FAR)
            row_sq[2 * i] = line[:, 0:sub]
            row_sq[2 * i + 1] = line[:, sub:big]
            if col_sq is not None:
                col = jnp.broadcast_to(jnp.sum(sq, 1, keepdims=True), (big, 128))
                col_sq[pl.ds(base, big), :] = jnp.where(iota((big, 128), 0) + base < n, col, FAR)
        return carry
    lax.fori_loop(0, (subs + 1) // 2, features, 0)

    fetch.wait()
    coef = [1.0 / jnp.full((8, 128), spread_ref[s], F32) / width for s in range(3)]
    rate = [c * math.log2(math.e) for c in coef]
    na = jnp.full((1, 128), jnp.maximum(n_own, 1).astype(F32), F32)
    nc = jnp.full((1, 128), jnp.maximum(n_oth, 1).astype(F32), F32)
    scale = float(bins * cap // 2 * width)
    k_self = jnp.concatenate([scale * (-(4.0 / (na * na)))] * 2, 1)
    k_cross = jnp.concatenate([scale * (4.0 / (na * nc))] * 2, 1)

    tot[...] = jnp.zeros_like(tot)
    w_ref[...] = jnp.zeros_like(w_ref)

    feats = (fx, fy)
    row_sqs = (srx, sry)

    def meet(which, rows, cols, base, col, at=0):
        xa = fx[pl.ds(base, rows), :]
        xb = feats[which][pl.ds(pl.multiple_of(col * sub, sub) + at, cols), :]
        inner[which, 0:rows, at:at + cols] = lax.dot_general(xa + xa, xb, NT, preferred_element_type=F32)

    def weigh(which, rows, cols, base, col, beside=()):
        steps = [(p, r) for p in range(0, cols, 128) for r in range(0, rows, 16)]
        beside = list(beside)
        every = max(1, len(steps) // (len(beside) + 1))
        total = jnp.zeros((8, 128), F32)
        for at, (p, r) in enumerate(steps):
            if beside and at % every == 0:
                beside.pop(0)()
            sb = row_sqs[which][col + p // sub, :, p % sub:p % sub + 128]
            parts = []
            for q in (r, r + 8):
                t = inner[which, q:q + 8, p:p + 128] - sax[pl.ds(base + q, 8), :] - sb
                e0 = jnp.exp2(t * rate[0])
                e1 = jnp.exp2(t * rate[1])
                e2 = jnp.exp2(t * rate[2])
                total = total + (e0 + e1 + e2)
                parts.append(e0 * coef[0] + e1 * coef[1] + e2 * coef[2])
            gram[which, r:r + 16, p:p + 128] = jnp.concatenate(parts, 0).astype(BF16)
        tot[which] += total
        for rest in beside:
            rest()

    def pull(which, rows, cols, col):
        xb = feats[which][pl.ds(pl.multiple_of(col * sub, sub), cols), :]
        acc[which, 0:rows, :] += jnp.dot(gram[which, 0:rows, 0:cols], xb, preferred_element_type=F32)

    def count(which, rows, cols):
        rsum[which, 0:rows, :] += jnp.dot(
            gram[which, 0:rows, 0:cols], jnp.ones((cols, 128), BF16), preferred_element_type=F32)

    def row_block(rows, base):
        acc[:, 0:rows, :] = jnp.zeros((2, rows, width), F32)
        rsum[:, 0:rows, :] = jnp.zeros((2, rows, 128), F32)
        blocks = subs // 2

        @pl.when(blocks > 0)
        def _():
            gram[1, 0:rows, :] = jnp.zeros((rows, big), BF16)
            meet(0, rows, big, base, 0)

            def turn(which, j, prev, later):
                other = 1 - which
                weigh(which, rows, big, base, 2 * j, [
                    lambda: meet(other, rows, sub, base, later, 0),
                    lambda: meet(other, rows, sub, base, later, sub),
                    lambda: pull(other, rows, big, prev),
                    lambda: count(other, rows, big)])

            def body(j, carry):
                turn(0, j, 2 * jnp.maximum(j - 1, 0), 2 * j)
                turn(1, j, 2 * j, 2 * jnp.minimum(j + 1, blocks - 1))
                return carry
            lax.fori_loop(0, blocks, body, 0)
            pull(1, rows, big, 2 * (blocks - 1))
            count(1, rows, big)

        @pl.when(subs % 2 == 1)
        def _():
            for which in (0, 1):
                meet(which, rows, sub, base, subs - 1)
            for which in (0, 1):
                weigh(which, rows, sub, base, subs - 1)
                pull(which, rows, sub, subs - 1)
                count(which, rows, sub)

        xf = fx[pl.ds(base, rows), :].astype(F32)
        force = [xf * jnp.concatenate([rsum[which, 0:rows, :]] * 2, 1) - acc[which, 0:rows, :] for which in (0, 1)]
        gz = (k_self * force[0] + k_cross * force[1]).astype(BF16)
        ge = lax.dot_general(gz, proj, NT, preferred_element_type=F32)
        gs[0, pl.ds(base, rows), :] = ge[:, :hw]
        gs[1, pl.ds(base, rows), :] = ge[:, hw:]
        emb = jnp.concatenate([xs[0, pl.ds(base, rows), :], xs[1, pl.ds(base, rows), :]], 1).astype(BF16)
        gw = lax.dot_general(emb, gz, TN, preferred_element_type=F32)
        w_ref[0, :width, :] += gw[:, :hw]
        w_ref[1, :width, :] += gw[:, hw:]

    def full(i, carry):
        row_block(big, pl.multiple_of(i * big, big))
        return carry
    lax.fori_loop(0, subs_own // 2, full, 0)

    @pl.when(subs_own % 2 == 1)
    def _():
        row_block(sub, pl.multiple_of((subs_own - 1) * sub, sub))

    for h in range(2):
        gs[h, pl.ds(n_own, cap), :] = jnp.zeros((cap, hw), F32)
    share = jnp.sum(tot[0], 0, keepdims=True) / (na * na) - jnp.sum(tot[1], 0, keepdims=True) / (na * nc)
    for h in range(2):
        w_ref[h, width:width + 8, :] = jnp.broadcast_to(share, (8, 128))
    off = 0
    for s in range(bins):
        out_ref[s, :, :hw] = gs[0, pl.ds(off, cap), :].astype(BF16)
        out_ref[s, :, hw:] = gs[1, pl.ds(off, cap), :].astype(BF16)
        off = off + cnt_ref[0, s]


def return_kernel(bins, reps, cap, slots, w_ref, ids_ref, g_out, w_out, l_out,
                  inbox, pick, p_recv, a_send, a_recv, zx, full, other,
                  send, recv, psem, asem, zsem, gsem, fsem, loc):
    z, me = lax.axis_index("dp"), lax.axis_index("bin")
    core = lax.rem(me, 2)
    q = lax.div(me, 2)
    chips = bins // 2
    sib = me + 1 - 2 * core
    jets = g_out.shape[0]
    width = g_out.shape[1]
    ar = width // chips
    tokens = float(jets * bins * reps)
    barrier = pltpu.get_barrier_semaphore()
    for k in range(1, bins):
        pl.semaphore_signal(barrier, inc=1, device_id=(z, lax.rem(me + k, bins)), device_id_type=MESH)
    for k in range(1, reps):
        pl.semaphore_signal(barrier, inc=1, device_id=(lax.rem(z + k, reps), me), device_id_type=MESH)

    place = slot_places(line_of(ids_ref), me, bins, cap)
    for first in range(0, jets, 128 if jets % 128 == 0 else jets):
        size = min(128, jets - first)
        part = jnp.broadcast_to(place[:, first:first + size], (size, size))
        column = jnp.sum(jnp.where(iota((size, size), 0) == iota((size, size), 1), part, 0), 1, keepdims=True)
        pick[first:first + size, :] = jnp.where(column == iota((size, bins * cap), 1), 1.0, 0.0).astype(BF16)
    pl.semaphore_wait(barrier, bins - 1 + reps - 1)

    def remote(src, dst, sems, dev):
        return pltpu.make_async_remote_copy(
            src_ref=src, dst_ref=dst, send_sem=sems.at[0], recv_sem=sems.at[1], device_id=dev, device_id_type=MESH)

    pair = remote(w_ref.at[1 - core], p_recv, psem, (z, sib))
    pair.start()

    def row_copy(k):
        dest = device_at(me, k, bins)
        return pltpu.make_async_remote_copy(
            src_ref=slots.at[dest], dst_ref=inbox.at[back(k, bins)], send_sem=send, recv_sem=recv,
            device_id=(z, dest), device_id_type=MESH)

    own = pltpu.make_async_copy(slots.at[me], inbox.at[0], loc)
    own.start()
    around = sorted(range(1, reps), key=lambda k: -hops(k, reps))

    pair.wait()
    loss_tile = w_ref[core, width:width + 1, :] + p_recv[width:width + 1, :]
    for k in range(chips):
        a_send[k, 0:ar, :] = w_ref[core, k * ar:(k + 1) * ar, :] + p_recv[k * ar:(k + 1) * ar, :]
        a_send[k, ar:ar + 1, :] = loss_tile

    others = [chip_at(q, dx, dy, bins) for dx, dy in plane_steps(bins) if dx or dy]
    for chip in others:
        remote(a_send.at[chip], a_recv.at[q], asem, (z, 2 * chip + core)).start()
    a_recv[q] = a_send[q]
    for k in turns(bins)[0:8]:
        row_copy(k).start()
    remote(a_send.at[pl.ds(0, chips - 1)], a_recv.at[pl.ds(0, chips - 1)], asem, (z, sib)).wait()
    for k in turns(bins)[8:24]:
        row_copy(k).start()
    chunk = a_recv[0]
    for k in range(1, chips):
        chunk = chunk + a_recv[k]
    zx[z] = chunk
    for k in around:
        remote(zx.at[z], zx.at[z], zsem, (lax.rem(z + k, reps), me)).start()
    remote(zx.at[pl.ds(0, reps - 1)], zx.at[pl.ds(0, reps - 1)], zsem, (z, sib)).wait()
    chunk = zx[0]
    for k in range(1, reps):
        chunk = chunk + zx[k]
    full[q] = chunk[0:ar, :] / tokens
    for chip in others:
        remote(full.at[q], full.at[q], gsem, (z, 2 * chip + core)).start()
    for k in turns(bins)[24:31]:
        row_copy(k).start()
    l_out[...] = jnp.broadcast_to(jnp.sum(chunk[ar:ar + 1, :], 1, keepdims=True) / reps, (1, 128))

    remote(full.at[pl.ds(0, chips - 1)], full.at[pl.ds(0, chips - 1)], gsem, (z, sib)).wait()
    last = remote(full, other, fsem, (z, sib))
    last.start()
    own.wait()
    pltpu.make_async_remote_copy(
        src_ref=slots.at[pl.ds(0, bins - 1)], dst_ref=inbox.at[pl.ds(1, bins - 1)], send_sem=send, recv_sem=recv,
        device_id=(z, sib), device_id_type=MESH).wait()
    g_out[...] = jnp.dot(pick[...], inbox[...].reshape(bins * cap, width), preferred_element_type=F32).astype(BF16)

    last.wait()
    here = full[...].reshape(width, 128)
    there = other[...].reshape(width, 128)
    w_out[:, 0:128] = jnp.where(core == 0, here, there)
    w_out[:, 128:256] = jnp.where(core == 0, there, here)


def vmem(count):
    return [pl.BlockSpec(memory_space=pltpu.VMEM)] * count


def local(embeddings, bin_ids, spreads, projection):
    jets, width = embeddings.shape
    bins, reps = lax.axis_size("bin"), lax.axis_size("dp")
    cap = 2 * jets // bins
    most = bins * cap
    chips = bins // 2
    ids = bin_ids.reshape(-1, 128) if jets % 128 == 0 else bin_ids.reshape(1, jets)
    dma = pltpu.SemaphoreType.DMA
    box = jax.ShapeDtypeStruct((bins, cap, width), BF16)
    limit = 48 << 20
    tally = jax.ShapeDtypeStruct((1, 128), jnp.int32)
    inbox, pinbox, counts, pcounts = pl.pallas_call(
        functools.partial(scatter_kernel, bins, cap),
        out_shape=(box, box, tally, tally),
        in_specs=vmem(2), out_specs=tuple(vmem(4)),
        scratch_shapes=[
            pltpu.VMEM((bins, cap, width), BF16),
            dma, dma((bins,)), dma, dma, dma((2,)), dma],
        compiler_params=pltpu.CompilerParams(collective_id=0, has_side_effects=True, vmem_limit_bytes=limit),
        name="scatter",
    )(embeddings, ids)

    big = 512
    top = -(-most // big) * big
    room = top + big
    slots, w_part = pl.pallas_call(
        functools.partial(pair_kernel, bins, cap, big),
        out_shape=(box, jax.ShapeDtypeStruct((2, width + 8, 128), F32)),
        in_specs=[pl.BlockSpec(memory_space=pltpu.SMEM)] * 2 + [pl.BlockSpec(memory_space=pltpu.HBM)] + vmem(3),
        out_specs=tuple(vmem(2)),
        scratch_shapes=[
            pltpu.SMEM((3,), F32), dma,
            pltpu.VMEM((2, room, width // 2), F32), pltpu.VMEM((2, room, width // 2), F32),
            pltpu.VMEM((2, room, width // 2), F32),
            pltpu.VMEM((top, width), BF16), pltpu.VMEM((top, width), BF16), pltpu.VMEM((top, 128), F32),
            pltpu.VMEM((2 * top // big, 8, big // 2), F32), pltpu.VMEM((2 * top // big, 8, big // 2), F32),
            pltpu.VMEM((2, big, big), F32), pltpu.VMEM((2, big, big), BF16),
            pltpu.VMEM((2, big, width), F32), pltpu.VMEM((2, big, 128), F32), pltpu.VMEM((2, 8, 128), F32)],
        compiler_params=pltpu.CompilerParams(vmem_limit_bytes=limit),
        name="pairs",
    )(counts, pcounts, spreads, projection, inbox, pinbox)

    ar = width // chips
    grad_emb, grad_w, loss = pl.pallas_call(
        functools.partial(return_kernel, bins, reps, cap),
        out_shape=(jax.ShapeDtypeStruct((jets, width), BF16), jax.ShapeDtypeStruct((width, width), F32),
                   jax.ShapeDtypeStruct((1, 128), F32)),
        in_specs=vmem(3), out_specs=tuple(vmem(3)),
        scratch_shapes=[
            pltpu.VMEM((bins, cap, width), BF16), pltpu.VMEM((jets, most), BF16),
            pltpu.VMEM((width + 8, 128), F32),
            pltpu.VMEM((chips, ar + 1, 128), F32), pltpu.VMEM((chips, ar + 1, 128), F32),
            pltpu.VMEM((reps, ar + 1, 128), F32), pltpu.VMEM((chips, ar, 128), F32), pltpu.VMEM((chips, ar, 128), F32),
            dma, dma, dma((2,)), dma((2,)), dma((2,)), dma((2,)), dma((2,)), dma],
        compiler_params=pltpu.CompilerParams(collective_id=1, has_side_effects=True, vmem_limit_bytes=limit),
        name="giveback",
    )(slots, w_part, ids)
    return grad_emb, grad_w, loss[0, 0]


def solution(mesh):
    return jax.shard_map(
        local,
        mesh=mesh,
        in_specs=(P(("dp", "bin"), None), P(("dp", "bin")), P(), P()),
        out_specs=(P(("dp", "bin"), None), P(), P()),
        check_vma=False,
    )
```
